256 devices in a mesh: date: 16 (over x, y_hi, core), rng: 16 (over z, y_lo).
Axes of the slice: x: 4, y: 4 (y_hi: 2, y_lo: 2; y = y_hi * 2 + y_lo), z: 8, core: 2. Of those that a mesh axis runs over, the one named last changes fastest.
Arguments:
- slave_complex_pixels: bfloat16 [32, 2, 128, 4096], P(None, None, 'date', 'rng')
- along_track_line_groups: int32 [32, 16, 64], P(None, 'rng'), may hold values from 0 to 126, as said below
- master_epoch_position: int32 [1], replicated, may hold values from 0 to 31
- sweep_identifier: int32 [64], replicated, may hold values from 0 to 1, never falling along the last dimension, each value on 1 to 48 neighbouring positions
- initial_filter_kernel: float32 [32, 5, 3, 3], replicated, may hold values from -0.875 to 0.875
- initial_filter_shift: float32 [32], replicated, may hold values from -3 to 3
- latter_filter_kernel: float32 [2, 32, 3, 3], replicated, may hold values from -0.375 to 0.375
- latter_filter_shift: float32 [2], replicated, may hold values from -3 to 3
Outputs:
- burn_logits: float32 [32, 2, 64, 4096], P('date', None, None, 'rng')
The draws below stay inside these ranges and needn't reach their ends.
Inputs may be any that keep to these rules, and one draw needn't show every extreme that they name: along_track_line_groups[d, g] is strictly increasing: the ingested rows that give the 64 window rows of date d in range segment g. `sweep_identifier`: burst never falls along the rows; each burst holds between 16 and 48 rows.
All inputs are finite; a program needn't handle non-finite values.
Results may differ from the reference program's by a relative error of at most 0.0003.
Values may be sent and summed in bfloat16 or wider, within the bound.
No kernel may reach another device: no remote copies, remote signals or barrier semaphores. Data moves between devices by JAX's collectives and lax.ppermute only.
A program may use at most 128 MiB of HBM per device.

```python
import math
import jax
import jax.numpy as jnp
import numpy as np
from jax import lax

ALONG_TRACK_LINES = 64
W_DEV = 256
CH_IN = 5
CH_MID = 32
CH_OUT = 2
BOX_AZ = 7
BOX_RG = 28
DATES = 32
SEGS = 16
NR = 4096
SRC_AZ = 128


def lists_from(key):
    base_key = jax.random.fold_in(key, 11)
    key_list = jax.random.split(base_key, 4)
    midway_line_number = ALONG_TRACK_LINES // 2
    offsets = jax.random.randint(key_list[0], (DATES * SEGS,), 0, midway_line_number + 1)
    skip_by = jax.random.randint(key_list[1], (DATES * SEGS,), 0, midway_line_number + 1)
    low_pick = jax.random.randint(key_list[2], (), 0, DATES * SEGS)
    high_pick = (low_pick + 1 + jax.random.randint(key_list[3], (), 0, DATES * SEGS - 1)) % (DATES * SEGS)
    offsets = offsets.at[low_pick].set(0).at[high_pick].set(midway_line_number).reshape(DATES, SEGS)
    skip_by = skip_by.at[high_pick].set(midway_line_number).reshape(DATES, SEGS)
    position = jnp.arange(ALONG_TRACK_LINES, dtype=jnp.int32)
    return (offsets[:, :, None] + position + position * skip_by[:, :, None] // ALONG_TRACK_LINES).astype(jnp.int32)


def draw_along_track_line_groups(key, part):
    return lists_from(key)


def draw_slave_complex_pixels(key, part):
    row_index = lists_from(key)
    key_list = jax.random.split(jax.random.fold_in(key, 23), 6)
    shape_all = (DATES, 2, SRC_AZ, NR)
    shape_win = (DATES, 2, ALONG_TRACK_LINES, NR)
    noise_all = jax.random.normal(key_list[0], shape_all, jnp.float32)
    scene_sig = jax.random.normal(key_list[1], (2, ALONG_TRACK_LINES, NR), jnp.float32)
    own_part = jax.random.normal(key_list[2], shape_win, jnp.float32)
    spread = 0.5 * math.log(10.0)
    row_scale = jnp.exp(jax.random.uniform(key_list[3], (ALONG_TRACK_LINES, 1), jnp.float32, 0.0, spread))
    col_scale = jnp.exp(jax.random.uniform(key_list[4], (1, NR), jnp.float32, 0.0, spread))
    mixing = jax.random.uniform(key_list[5], (DATES, 1, 1, 1), jnp.float32, 0.1, 0.95)
    window = (jnp.sqrt(mixing) * scene_sig[None] + jnp.sqrt(1.0 - mixing) * own_part) * row_scale * col_scale
    cube_src = jnp.moveaxis(noise_all.reshape(DATES, 2, SRC_AZ, SEGS, W_DEV), 3, 1)
    values = jnp.moveaxis(window.reshape(DATES, 2, ALONG_TRACK_LINES, SEGS, W_DEV), 3, 1)
    placed = jax.vmap(jax.vmap(lambda target, rows_here, given: target.at[:, rows_here, :].set(given)))(cube_src, row_index, values)
    return jnp.moveaxis(placed, 1, 3).reshape(shape_all).astype(jnp.bfloat16)


def profile(count, total, limit, lean):
    weights = [(1 << 20) // math.isqrt(grade ** lean) + 1 for grade in range(2, count + 1)]
    spare, given = total - limit - (count - 1), [1] * (count - 1)
    while spare > 0:
        movable = [i for i in range(count - 1) if given[i] < limit]
        mass, budget = sum([weights[i] for i in movable]), spare
        for i in movable:
            more = min(limit - given[i], max(1, budget * weights[i] // mass), spare)
            given[i] = given[i] + more
            spare = spare - more
    return np.array([limit] + given)


def uneven(own_key, count, total, limit, lean):
    if count == 2:
        one = jax.random.randint(own_key, (), max(1, total - limit), min(limit, total - 1) + 1)
        return jnp.stack([one, total - one])
    tallies = jnp.asarray(profile(count, total, limit, lean), jnp.int32)
    twos = (count - 1) // 2
    source_of, sink = tallies[1:1 + 2 * twos:2], tallies[2:2 + 2 * twos:2]
    room = jnp.minimum(source_of - 1, limit - sink)
    shifted = jax.random.randint(jax.random.fold_in(own_key, 1), (twos,), 0, 1 << 20) % (room + 1)
    tallies = tallies.at[1:1 + 2 * twos:2].set(source_of - shifted).at[2:2 + 2 * twos:2].set(sink + shifted)
    return tallies[jax.random.permutation(jax.random.fold_in(own_key, 2), count)]


def gaussian(stream_key, dims, deviation, most, held_as=jnp.bfloat16):
    array = deviation * jax.random.normal(stream_key, dims, jnp.float32)
    return jnp.clip(array, min=-most, max=most).astype(held_as)


def setup_inputs(seed: int = 0) -> dict:
    splits = jax.random.split(jax.random.key(seed), 9)
    slave_complex_pixels = draw_slave_complex_pixels(jax.random.fold_in(splits[8], 71), 0)
    along_track_line_groups = draw_along_track_line_groups(jax.random.fold_in(splits[8], 71), 0)
    master_epoch_position = jax.random.randint(splits[2], (1,), 0, DATES).astype(jnp.int32)
    sweep_identifier = jnp.searchsorted(jnp.cumsum(uneven(splits[3], 2, ALONG_TRACK_LINES, 3 * ALONG_TRACK_LINES // 4, 0)), jnp.arange(ALONG_TRACK_LINES), side="right").astype(jnp.int32)
    initial_filter_kernel = gaussian(splits[4], (CH_MID, CH_IN, 3, 3), (CH_IN * 9) ** -0.5, 0.875, jnp.float32)
    initial_filter_shift = gaussian(splits[5], (CH_MID,), 0.5, 3.0, jnp.float32)
    latter_filter_kernel = gaussian(splits[6], (CH_OUT, CH_MID, 3, 3), (CH_MID * 9) ** -0.5, 0.375, jnp.float32)
    latter_filter_shift = gaussian(splits[7], (CH_OUT,), 1.0, 3.0, jnp.float32)
    return dict(slave_complex_pixels=slave_complex_pixels, along_track_line_groups=along_track_line_groups, master_epoch_position=master_epoch_position, sweep_identifier=sweep_identifier, initial_filter_kernel=initial_filter_kernel, initial_filter_shift=initial_filter_shift, latter_filter_kernel=latter_filter_kernel, latter_filter_shift=latter_filter_shift)


HIGH = lax.Precision.HIGHEST
EPSILON = 1e-06

def pick_rows(one_frame, row_index):
    return jnp.take(one_frame, row_index.astype(jnp.int32), axis=1)

def coregister(slave_complex_pixels, along_track_line_groups):
    cube_src = slave_complex_pixels.reshape(DATES, 2, SRC_AZ, SEGS, W_DEV)
    cube_src = jnp.moveaxis(cube_src, 3, 1)
    picked = jax.vmap(jax.vmap(pick_rows))(cube_src, along_track_line_groups)
    return jnp.moveaxis(picked, 1, 3).reshape(DATES, 2, ALONG_TRACK_LINES, NR)

def make_channels(ref_re, ref_im, sec_re, sec_im):
    pow_ref = jnp.broadcast_to(ref_re * ref_re + ref_im * ref_im, sec_re.shape)
    pow_sec = sec_re * sec_re + sec_im * sec_im
    cross_re = ref_re * sec_re + ref_im * sec_im
    cross_im = ref_im * sec_re - ref_re * sec_im
    return jnp.stack([pow_ref, pow_sec, cross_re, cross_im, jnp.sqrt(pow_ref * pow_sec)])

def features(moving_averaged):
    denominator = jnp.sqrt(moving_averaged[0] * moving_averaged[1]) + EPSILON
    return jnp.stack([moving_averaged[2] / denominator, moving_averaged[3] / denominator, moving_averaged[4] / denominator, jnp.log(moving_averaged[1] + EPSILON) - jnp.log(moving_averaged[0] + EPSILON), jnp.log(moving_averaged[0] / (BOX_AZ * BOX_RG) + EPSILON)])

def slant_accumulated(layered_planes):
    across_track_number = layered_planes.shape[2]
    left_pad = BOX_RG // 2
    bordered_patch = jnp.pad(layered_planes, ((0, 0), (0, 0), (left_pad, BOX_RG - 1 - left_pad)))
    cumulative_tally = jnp.zeros(layered_planes.shape, jnp.float32)
    for line_displacement in range(BOX_RG):
        cumulative_tally = cumulative_tally + bordered_patch[:, :, line_displacement:line_displacement + across_track_number]
    return cumulative_tally

def along_track_accumulated(slant_averaged, sweep_identifier):
    midway_line_number = (BOX_AZ - 1) // 2
    bordered_patch = jnp.pad(slant_averaged, ((0, 0), (midway_line_number, midway_line_number), (0, 0)))
    sweep_border_fill = jnp.pad(sweep_identifier, (midway_line_number, midway_line_number), constant_values=-1)
    cumulative_tally = jnp.zeros(slant_averaged.shape, jnp.float32)
    for line_displacement in range(BOX_AZ):
        inside_identical_sweep = (sweep_border_fill[line_displacement:line_displacement + ALONG_TRACK_LINES] == sweep_identifier).astype(jnp.float32)
        cumulative_tally = cumulative_tally + bordered_patch[:, line_displacement:line_displacement + ALONG_TRACK_LINES, :] * inside_identical_sweep[None, :, None]
    return cumulative_tally

def conv_taps(field, weights, biases):
    along_track_lines_number = field.shape[2]
    across_track_number = field.shape[3] - 2
    bordered_patch = jnp.pad(field, ((0, 0), (0, 0), (1, 1), (0, 0)))
    cumulative_tally = jnp.zeros((weights.shape[0], field.shape[1], along_track_lines_number, across_track_number), jnp.float32) + biases[:, None, None, None]
    for tap_a in range(3):
        for tap_b in range(3):
            cumulative_tally = cumulative_tally + jnp.einsum('oi,inpw->onpw', weights[:, :, tap_a, tap_b], bordered_patch[:, :, tap_a:tap_a + along_track_lines_number, tap_b:tap_b + across_track_number], precision=HIGH)
    return cumulative_tally

def conv_same(field, weights, biases):
    bordered_patch = jnp.pad(field, ((0, 0), (0, 0), (1, 1)))
    return conv_taps(bordered_patch[:, None], weights, biases)[:, 0]

def reference(slave_complex_pixels, along_track_line_groups, master_epoch_position, sweep_identifier, initial_filter_kernel, initial_filter_shift, latter_filter_kernel, latter_filter_shift):
    frames = coregister(slave_complex_pixels, along_track_line_groups)
    chosen = master_epoch_position[0].astype(jnp.int32)
    ref_frame = lax.dynamic_index_in_dim(frames, chosen, 0, keepdims=False).astype(jnp.float32)

    def one_date(frame_bf):
        sec_frame = frame_bf.astype(jnp.float32)
        layered_planes = make_channels(ref_frame[0], ref_frame[1], sec_frame[0], sec_frame[1])
        moving_averaged = along_track_accumulated(slant_accumulated(layered_planes), sweep_identifier)
        descriptor_lattice = features(moving_averaged)
        hidden = jax.nn.relu(conv_same(descriptor_lattice, initial_filter_kernel, initial_filter_shift))
        return conv_same(hidden, latter_filter_kernel, latter_filter_shift)
    return lax.map(one_date, frames)
```

```python
import jax
import jax.numpy as jnp
from jax import lax
from jax.experimental import pallas as pl
from jax.experimental.pallas import tpu as pltpu
from jax.sharding import PartitionSpec as P

BOX_AZ = 7
BOX_RG = 28
EPSILON = 1e-06
ROWS = 64
COLS = 256
BANDS = 16
EDGE = 16
BLOCKS = 8
TAPS = 240
F32 = jnp.float32
BF16 = jnp.bfloat16


def iota(shape, dim):
    return lax.broadcasted_iota(jnp.int32, shape, dim)


def halves(value):
    high = value.astype(BF16)
    return high, (value - high.astype(F32)).astype(BF16)


def matmul(left, right):
    return jnp.dot(left, right, preferred_element_type=F32)


def spread_kernel(first_ref, second_ref, first_out, second_out):
    row, col = iota((256, TAPS), 0), iota((256, TAPS), 1)
    tap = col % 16 - row % 8 - 3
    widen = (iota((256, 32), 0) // 8 == iota((256, 32), 1)).astype(BF16)
    source, target = iota((48, TAPS), 0), iota((48, TAPS), 1)
    base = (target % 80) // 16 * 9 + target // 80
    for part, piece in enumerate(halves(first_ref[...])):
        tall = matmul(widen, piece).astype(BF16)
        offset = ((source == 45) & (target == 0)).astype(BF16)
        spread = matmul(tall, offset)
        for a in range(3):
            chosen = (source == base + 3 * a).astype(BF16)
            spread = jnp.where(tap == a, matmul(tall, chosen), spread)
        first_out[256 * part : 256 * part + 256, :] = spread.astype(BF16)
    row, col = iota((64, 256), 0), iota((64, 256), 1)
    out_row = jnp.where(row < 48, row % 8, jnp.where(row < 54, -1, 8))
    tap = col % 8 - out_row + 1
    to_row, from_row = iota((64, 24), 0), iota((64, 24), 1)
    group = jnp.where(to_row < 48, to_row // 8, (to_row - 48) % 6)
    real = to_row < 60
    widen = (iota((32, 256), 1) // 8 == iota((32, 256), 0)).astype(BF16)
    for part, piece in enumerate(halves(second_ref[...])):
        wide = matmul(piece, widen).astype(BF16)
        spread = jnp.zeros((64, 256), F32)
        for a in range(3):
            chosen = (real & (from_row == group + 6 * a)).astype(BF16)
            spread = jnp.where(tap == a, matmul(chosen, wide), spread)
        second_out[64 * part : 64 * part + 64, :] = spread.astype(BF16)


def pick_kernel(chosen_ref, bands_ref, window_ref, first_ref, last_ref):
    lane = iota((ROWS, 128), 1)
    first = jnp.zeros((ROWS, 128), F32)
    last = jnp.zeros((ROWS, 128), F32)
    for slot in range(3):
        for part in range(2):
            k = 2 * slot + part
            rows = bands_ref[:, slot, part].astype(F32).reshape(8 * BANDS, COLS).astype(BF16)
            picked = matmul(chosen_ref[slot], rows)
            window_ref[slot, part] = picked.astype(BF16)
            here = (lane >= EDGE * k) & (lane < EDGE * (k + 1))
            left = picked[:, :128]
            right = pltpu.roll(picked[:, 128:], EDGE * (k + 1), 1)
            if k:
                left = pltpu.roll(left, EDGE * k, 1)
            first = jnp.where(here, left, first)
            last = jnp.where(here, right, last)
    first_ref[...] = first.astype(BF16)
    last_ref[...] = last.astype(BF16)


def products(re, im):
    ref_re, ref_im = re[2], im[2]
    pow_ref = ref_re * ref_re + ref_im * ref_im
    pow_sec = [re[d] * re[d] + im[d] * im[d] for d in range(2)]
    cross_re = [ref_re * re[d] + ref_im * im[d] for d in range(2)]
    cross_im = [ref_im * re[d] - ref_re * im[d] for d in range(2)]
    both = [jnp.sqrt(pow_ref * pow_sec[d]) for d in range(2)]
    return pow_ref, pow_sec, cross_re, cross_im, both


def sum_rows(summed, near_ref):
    high, low = halves(summed)
    return matmul(near_ref[...], jnp.concatenate([high, low], axis=0))


def features(boxed, log_ref, inside):
    inverse = 1.0 / (jnp.sqrt(boxed[0] * boxed[1]) + EPSILON)
    mean_log = jnp.log(boxed[0] / (BOX_AZ * BOX_RG) + EPSILON)
    return [
        boxed[2] * inverse,
        boxed[3] * inverse,
        boxed[4] * inverse,
        jnp.log(boxed[1] + EPSILON) - log_ref,
        jnp.where(inside, mean_log, 0.0),
    ]


def window_rows(width):
    row = iota((16 * BLOCKS, width), 0)
    frame_row = row // 16 * 8 - 4 + row % 16
    return (frame_row >= 0) & (frame_row < ROWS), row % 16 == 0


def store_taps(taken, first_row, high_ref, low_ref):
    width = taken[0].shape[1]
    for i, field in enumerate(taken):
        for b in range(3):
            moved = field if b == 1 else pltpu.roll(field, (1, 0, width - 1)[b], 1)
            if i == 0 and b == 0:
                moved = jnp.where(first_row, 1.0, moved)
            high, low = halves(moved)
            for j in range(BLOCKS):
                at = b * 80 + i * 16
                high_ref[j, at : at + 16, :] = high[16 * j : 16 * j + 16]
                low_ref[j, at : at + 16, :] = low[16 * j : 16 * j + 16]


def head_block(high, low, first_ref, second_ref, inside):
    doubled = matmul(first_ref[...], high)
    hidden = doubled[:256] + doubled[256:] + matmul(first_ref[:256, :], low)
    hidden = jnp.maximum(hidden, 0.0)
    if inside is not None:
        hidden = jnp.where(inside, hidden, 0.0)
    high, low = halves(hidden)
    doubled = matmul(second_ref[...], high)
    return doubled[:64] + doubled[64:] + matmul(second_ref[:64, :], low)


def joined(parts, j, group):
    width = parts[j].shape[1]
    row = iota((8, width), 0)
    value = parts[j][8 * group : 8 * group + 8]
    if j:
        below = parts[j - 1][54 + group : 55 + group]
        value = value + jnp.where(row == 0, below, 0.0)
    if j + 1 < BLOCKS:
        above = parts[j + 1][48 + group : 49 + group]
        value = value + jnp.where(row == 7, above, 0.0)
    return value


def class_rows(parts, j, o, shift_ref):
    width = parts[j].shape[1]
    before = pltpu.roll(joined(parts, j, o), 1, 1)
    after = pltpu.roll(joined(parts, j, 4 + o), width - 1, 1)
    return before + joined(parts, j, 2 + o) + after + shift_ref[o]


def middle_kernel(shift_ref, window_ref, near_ref, first_ref, second_ref, out_ref, high_ref, low_ref):
    re = [window_ref[s, 0].astype(F32) for s in range(3)]
    im = [window_ref[s, 1].astype(F32) for s in range(3)]
    pow_ref, pow_sec, cross_re, cross_im, both = products(re, im)
    gap = iota((COLS, COLS), 0) - iota((COLS, COLS), 1) + BOX_RG // 2
    band = ((gap >= 0) & (gap < BOX_RG)).astype(BF16)
    band = jnp.concatenate([band, band], axis=0)
    inside, first_row = window_rows(COLS)

    def boxed(plane):
        summed = matmul(jnp.concatenate(halves(plane), axis=1), band)
        return sum_rows(summed, near_ref)

    box_ref = boxed(pow_ref)
    log_ref = jnp.log(box_ref + EPSILON)
    for d in range(2):
        sums = [box_ref] + [boxed(p[d]) for p in (pow_sec, cross_re, cross_im, both)]
        store_taps(features(sums, log_ref, inside), first_row, high_ref.at[d], low_ref.at[d])
    for d in range(2):
        parts = [
            head_block(high_ref[d, j], low_ref[d, j], first_ref, second_ref, None) for j in range(BLOCKS)
        ]
        for j in range(BLOCKS):
            for o in range(2):
                out_ref[d, o, 8 * j : 8 * j + 8, :] = class_rows(parts, j, o, shift_ref)


def edge_kernel(
    place_ref, shift_ref, window_ref, before_ref, after_ref, near_ref, first_ref, second_ref, done_ref,
    out_ref, high_ref, low_ref,
):
    lane = iota((ROWS, 128), 1)
    before, after = before_ref[...].astype(F32), after_ref[...].astype(F32)

    def pixels(slot, part):
        k = 2 * slot + part
        value = window_ref[slot, part].astype(F32)
        own_first = pltpu.roll(value[:, :128], EDGE, 1)
        own_last = pltpu.roll(value[:, 128:], 96, 1)
        left = pltpu.roll(before, 128 - EDGE * k, 1) if k else before
        right = pltpu.roll(after, (96 - EDGE * k) % 128, 1) if k != 6 else after
        tile = jnp.where(lane < EDGE, left, own_first)
        tile = jnp.where(lane < 64, tile, own_last)
        tile = jnp.where(lane < 96, tile, right)
        return jnp.where(lane < 112, tile, 0.0)

    re = [pixels(s, 0) for s in range(3)]
    im = [pixels(s, 1) for s in range(3)]
    pow_ref, pow_sec, cross_re, cross_im, both = products(re, im)
    source, target = iota((128, 128), 0), iota((128, 128), 1)
    from_col = jnp.where(source < 64, source - 16, source + 160)
    side = target % 64 // 32
    to_col = target % 32 + jnp.where(side == 0, -4, 232)
    gap = from_col - to_col + BOX_RG // 2
    near = (gap >= 0) & (gap < BOX_RG) & (source // 64 == side)
    bands = [(near & (target // 64 == d)).astype(BF16) for d in range(2)]
    band = jnp.concatenate([bands[0], bands[0], bands[1], bands[1]], axis=0)

    def boxed(planes):
        pieces = halves(planes[0]) + halves(planes[1])
        return sum_rows(matmul(jnp.concatenate(pieces, axis=1), band), near_ref)

    inside, first_row = window_rows(128)
    place = place_ref[0]

    def in_frame(rows):
        spot = iota((rows, 128), 1)
        column = spot % 32 + jnp.where(spot % 64 < 32, -4, 232)
        low = jnp.where(place == 0, 0, -128)
        high = jnp.where(place == place_ref[1] - 1, COLS, 2 * COLS)
        return (column >= low) & (column < high)

    valid = in_frame(16 * BLOCKS)
    sums = [boxed([pow_ref, pow_ref])] + [boxed(p) for p in (pow_sec, cross_re, cross_im, both)]
    taken = features(sums, jnp.log(sums[0] + EPSILON), inside)
    store_taps([jnp.where(valid, f, 0.0) for f in taken], first_row, high_ref, low_ref)
    kept = in_frame(256)
    parts = [head_block(high_ref[j], low_ref[j], first_ref, second_ref, kept) for j in range(BLOCKS)]
    spot = iota((8, 128), 1)
    for j in range(BLOCKS):
        for o in range(2):
            value = class_rows(parts, j, o, shift_ref)
            at = slice(8 * j, 8 * j + 8)
            for d in range(2):
                left = pltpu.roll(value, 128 - 64 * d - 4, 1)
                right = pltpu.roll(value, (112 - 64 * d - 40) % 128, 1)
                out_ref[d, o, at, :128] = jnp.where(spot < EDGE, left, done_ref[d, o, at, :128])
                out_ref[d, o, at, 128:] = jnp.where(spot >= 112, right, done_ref[d, o, at, 128:])


def vmem():
    return pl.BlockSpec(memory_space=pltpu.VMEM)


def smem():
    return pl.BlockSpec(memory_space=pltpu.SMEM)


def local(
    slave_complex_pixels,
    along_track_line_groups,
    master_epoch_position,
    sweep_identifier,
    initial_filter_kernel,
    initial_filter_shift,
    latter_filter_kernel,
    latter_filter_shift,
):
    date_index = lax.axis_index("date")
    rng_count = lax.axis_size("rng")
    chosen = master_epoch_position[0]
    own = slave_complex_pixels.reshape(BANDS, 2, 2, 8, COLS)
    master = lax.dynamic_slice_in_dim(slave_complex_pixels, chosen, 1, 0)[None]
    sent = jnp.concatenate([own, jnp.broadcast_to(master, (BANDS, 1, 2, 8, COLS))], axis=1)
    bands = lax.all_to_all(sent, "date", split_axis=0, concat_axis=0, tiled=True)

    lists = along_track_line_groups[:, 0, :]
    mine = lax.dynamic_slice_in_dim(lists, date_index * 2, 2, 0)
    lists = jnp.concatenate([mine, lax.dynamic_slice_in_dim(lists, chosen, 1, 0)], axis=0)
    row_of = lax.broadcasted_iota(jnp.int32, (3, ROWS, 8 * BANDS), 2)
    picks = (lists[:, :, None] == row_of).astype(BF16)

    window = jnp.arange(16 * BLOCKS)
    frame_row = window // 16 * 8 - 4 + window % 16
    row_id = jnp.arange(ROWS)
    burst = sweep_identifier.astype(jnp.int32)
    target_burst = jnp.where(window // 16 * 8 - 4 + window % 16 < 0, -1, 0) + jnp.sum(
        jnp.where(frame_row[:, None] == row_id[None, :], burst[None, :], 0), axis=1
    )
    near = (
        (jnp.abs(row_id[None, :] - frame_row[:, None]) <= BOX_AZ // 2)
        & (burst[None, :] == target_burst[:, None])
        & (frame_row >= 0)[:, None]
        & (frame_row < ROWS)[:, None]
    ).astype(BF16)
    near = jnp.concatenate([near, near], axis=1)

    first = jnp.concatenate(
        [
            initial_filter_kernel.reshape(32, 45),
            initial_filter_shift[:, None],
            jnp.zeros((32, 2), F32),
        ],
        axis=1,
    )
    second = jnp.pad(jnp.transpose(latter_filter_kernel, (2, 3, 0, 1)).reshape(18, 32), ((0, 6), (0, 0)))
    first_spread, second_spread = pl.pallas_call(
        spread_kernel,
        out_shape=(
            jax.ShapeDtypeStruct((512, TAPS), BF16),
            jax.ShapeDtypeStruct((128, 256), BF16),
        ),
        in_specs=[vmem()] * 2,
        out_specs=(vmem(), vmem()),
        cost_estimate=pl.CostEstimate(flops=10**7, bytes_accessed=10**6, transcendentals=0),
    )(first, second)

    pixels, first_edge, last_edge = pl.pallas_call(
        pick_kernel,
        out_shape=(
            jax.ShapeDtypeStruct((3, 2, ROWS, COLS), BF16),
            jax.ShapeDtypeStruct((ROWS, 128), BF16),
            jax.ShapeDtypeStruct((ROWS, 128), BF16),
        ),
        in_specs=[vmem()] * 2,
        out_specs=(vmem(),) * 3,
    )(picks, bands)

    up = [(i, i + 1) for i in range(rng_count - 1)]
    down = [(i + 1, i) for i in range(rng_count - 1)]
    before = lax.ppermute(last_edge, "rng", up)
    after = lax.ppermute(first_edge, "rng", down)

    middle = pl.pallas_call(
        middle_kernel,
        out_shape=jax.ShapeDtypeStruct((2, 2, ROWS, COLS), F32),
        in_specs=[smem()] + [vmem()] * 4,
        out_specs=vmem(),
        scratch_shapes=[
            pltpu.VMEM((2, BLOCKS, TAPS, COLS), BF16),
            pltpu.VMEM((2, BLOCKS, TAPS, COLS), BF16),
        ],
        cost_estimate=pl.CostEstimate(flops=4 * 10**9, bytes_accessed=10**7, transcendentals=10**5),
    )(latter_filter_shift, pixels, near, first_spread, second_spread)

    place = jnp.stack([lax.axis_index("rng"), jnp.int32(rng_count)]).astype(jnp.int32)
    return pl.pallas_call(
        edge_kernel,
        out_shape=jax.ShapeDtypeStruct((2, 2, ROWS, COLS), F32),
        in_specs=[smem()] * 2 + [vmem()] * 7,
        out_specs=vmem(),
        scratch_shapes=[
            pltpu.VMEM((BLOCKS, TAPS, 128), BF16),
            pltpu.VMEM((BLOCKS, TAPS, 128), BF16),
        ],
        input_output_aliases={8: 0},
    )(place, latter_filter_shift, pixels, before, after, near, first_spread, second_spread, middle)


def solution(mesh):
    placed = (P(None, None, "date", "rng"), P(None, "rng", None), P(), P(), P(), P(), P(), P())
    return jax.shard_map(
        local, mesh=mesh, in_specs=placed, out_specs=P("date", None, None, "rng"), check_vma=False
    )
```

```python
import jax
import jax.numpy as jnp
from jax import lax
from jax.experimental import pallas as pl
from jax.experimental.pallas import tpu as pltpu
from jax.sharding import PartitionSpec as P

BOX_AZ = 7
BOX_RG = 28
EPSILON = 1e-06
ROWS = 64
COLS = 256
BANDS = 16
EDGE = 16
STEP = 6
BLOCKS = 11
WINDOWS = 12
HIDDEN = 32
WIDE = STEP * HIDDEN
F32 = jnp.float32
BF16 = jnp.bfloat16


def iota(shape, dim):
    return lax.broadcasted_iota(jnp.int32, shape, dim)


def halves(value):
    high = value.astype(BF16)
    return high, (value - high.astype(F32)).astype(BF16)


def matmul(left, right):
    return jnp.dot(left, right, preferred_element_type=F32)


def send_kernel(chosen_ref, own_ref, sent_ref):
    chosen = chosen_ref[0]
    sent_ref[:, :2] = own_ref[...]
    master = own_ref[chosen // 2, chosen % 2]
    for band in range(BANDS):
        sent_ref[band, 2] = master


def spread_kernel(first_ref, second_ref, shift_ref, first_out, second_out, shift_out):
    row, col = iota((WIDE, 128), 0), iota((WIDE, 128), 1)
    tap = col % 8 - row // HIDDEN
    widen = (iota((WIDE, HIDDEN), 0) % HIDDEN == iota((WIDE, HIDDEN), 1)).astype(BF16)
    source, target = iota((48, 128), 0), iota((48, 128), 1)
    piece = target // 8
    shift = jnp.where(piece < 6, piece // 2, jnp.where(piece < 12, piece // 2 - 3, piece - 12))
    feature = jnp.where(piece < 6, piece % 2, jnp.where(piece < 12, 2 + piece % 2, 4))
    base = feature * 9 + shift
    offset = ((source == 45) & (target == 120)).astype(BF16)
    taken = [((source == base + 3 * a) & (piece < 15)).astype(BF16) for a in range(3)]
    for part, half in enumerate(halves(first_ref[...])):
        tall = matmul(widen, half).astype(BF16)
        spread = jnp.zeros((WIDE, 128), F32)
        for a in range(3):
            spread = jnp.where(tap == a, matmul(tall, taken[a]), spread)
        at = slice(WIDE * part, WIDE * part + WIDE)
        first_out[at, :128] = (spread + matmul(tall, offset)).astype(BF16)
        first_out[at, 128:] = (spread if part == 0 else jnp.zeros_like(spread)).astype(BF16)
    row, col = iota((48, WIDE), 0), iota((48, WIDE), 1)
    tap = col // HIDDEN + 2 - row % 8
    widen = (iota((HIDDEN, WIDE), 1) % HIDDEN == iota((HIDDEN, WIDE), 0)).astype(BF16)
    group, source = iota((48, 24), 0) // 8, iota((48, 24), 1)
    for part, half in enumerate(halves(second_ref[...])):
        wide = matmul(half, widen).astype(BF16)
        spread = jnp.zeros((48, WIDE), F32)
        for a in range(3):
            chosen = (source == group + 6 * a).astype(BF16)
            spread = jnp.where(tap == a, matmul(chosen, wide), spread)
        second_out[48 * part : 48 * part + 48, :] = spread.astype(BF16)
    for o in range(2):
        shift_out[o] = jnp.full((8, 128), shift_ref[o], F32)


def pick_kernel(chosen_ref, bands_ref, window_ref, first_ref, last_ref):
    lane = iota((ROWS, 128), 1)
    first = jnp.zeros((ROWS, 128), F32)
    last = jnp.zeros((ROWS, 128), F32)
    for slot in range(3):
        for part in range(2):
            k = 2 * slot + part
            rows = bands_ref[:, slot, part].astype(F32).reshape(8 * BANDS, COLS).astype(BF16)
            picked = matmul(chosen_ref[slot], rows)
            window_ref[slot, part] = picked.astype(BF16)
            here = (lane >= EDGE * k) & (lane < EDGE * (k + 1))
            left = picked[:, :128]
            right = pltpu.roll(picked[:, 128:], EDGE * (k + 1), 1)
            if k:
                left = pltpu.roll(left, EDGE * k, 1)
            first = jnp.where(here, left, first)
            last = jnp.where(here, right, last)
    first_ref[...] = first.astype(BF16)
    last_ref[...] = last.astype(BF16)


def products(re, im):
    ref_re, ref_im = re[2], im[2]
    pow_ref = ref_re * ref_re + ref_im * ref_im
    planes = [pow_ref]
    for d in range(2):
        pow_sec = re[d] * re[d] + im[d] * im[d]
        planes += [
            pow_sec,
            ref_re * re[d] + ref_im * im[d],
            ref_im * re[d] - ref_re * im[d],
            jnp.sqrt(pow_ref * pow_sec),
        ]
    return planes


def sum_rows(summed, near_ref):
    return matmul(near_ref[...], jnp.concatenate(halves(summed), axis=0))


def mean_log(box_ref, inside):
    return jnp.where(inside, jnp.log(box_ref / (BOX_AZ * BOX_RG) + EPSILON), 0.0)


def features(box_ref, log_ref, boxed):
    inverse = 1.0 / (jnp.sqrt(box_ref * boxed[0]) + EPSILON)
    ratio = jnp.log(boxed[0] + EPSILON) - log_ref
    return boxed[1] * inverse, boxed[2] * inverse, boxed[3] * inverse, ratio


def window_rows(rows, base):
    row = iota(rows, 0)
    frame_row = row // 8 * STEP - 1 + row % 8 + base
    return (frame_row >= 0) & (frame_row < ROWS)


def sideways(value, b, span):
    if b == 1:
        return value
    width = value.shape[1]
    if span == width:
        return pltpu.roll(value, 1 if b == 0 else width - 1, 1)
    pieces = [sideways(value[:, at : at + span], b, span) for at in range(0, width, span)]
    return jnp.concatenate(pieces, axis=1)


def store_pieces(taps_ref, piece, upper, lower):
    for j in range(taps_ref.shape[0]):
        at = slice(8 * j, 8 * j + 8)
        high, low = halves(jnp.concatenate([upper[at], lower[at]], axis=0))
        taps_ref[j, 8 * piece : 8 * piece + 16, :] = high
        taps_ref[j, 128 + 8 * piece : 144 + 8 * piece, :] = low


def store_taps(taken, taps_ref, span):
    for pair in range(2):
        for b in range(3):
            upper, lower = [sideways(taken[2 * pair + k], b, span) for k in range(2)]
            store_pieces(taps_ref, 6 * pair + 2 * b, upper, lower)


def store_shared(shared, taps_refs, span):
    moved = [sideways(shared, b, span) for b in range(3)]
    one = jnp.where(iota(shared.shape, 0) % 8 == 0, 1.0, 0.0)
    for taps_ref in taps_refs:
        store_pieces(taps_ref, 12, moved[0], moved[1])
        store_pieces(taps_ref, 14, moved[2], one)


def head_block(taps, first_ref, second_ref, keep):
    doubled = matmul(first_ref[...], taps)
    hidden = jnp.maximum(doubled[:WIDE] + doubled[WIDE:], 0.0)
    high, low = halves(keep(hidden))
    doubled = matmul(second_ref[...], high)
    return doubled[:48] + doubled[48:] + matmul(second_ref[:48, :], low)


def class_window(parts, o, span):
    groups = [parts[16 * b + 8 * o : 16 * b + 8 * o + 8] for b in range(3)]
    return sum(sideways(groups[b], b, span) for b in range(3))


def carried(window, previous):
    if previous is None:
        return window
    row = iota(window.shape, 0)
    return window + jnp.where(row < 2, pltpu.roll(previous, 2, 0), 0.0)


def middle_kernel(window_ref, near_ref, first_ref, second_ref, shift_ref, out_ref, taps_ref, sum_ref):
    re = [window_ref[s, 0].astype(F32) for s in range(3)]
    im = [window_ref[s, 1].astype(F32) for s in range(3)]
    gap = iota((COLS, COLS), 0) - iota((COLS, COLS), 1) + BOX_RG // 2
    band = ((gap >= 0) & (gap < BOX_RG)).astype(BF16)
    planes = jnp.concatenate(products(re, im), axis=0)
    summed = matmul(jnp.concatenate(halves(planes), axis=1), jnp.concatenate([band, band], axis=0))
    live = 8 * BLOCKS
    boxed = [sum_rows(summed[ROWS * k : ROWS * k + ROWS], near_ref)[:live] for k in range(9)]
    log_ref = jnp.log(boxed[0] + EPSILON)
    shared = mean_log(boxed[0], window_rows((live, COLS), 0))
    store_shared(shared, [taps_ref.at[d] for d in range(2)], COLS)
    for d in range(2):
        store_taps(features(boxed[0], log_ref, boxed[1 + 4 * d : 5 + 4 * d]), taps_ref.at[d], COLS)

    def keep(j):
        def masked(hidden):
            if j < BLOCKS - 1:
                return hidden
            row = iota(hidden.shape, 0)
            return jnp.where(row < (ROWS - STEP * j) * HIDDEN, hidden, 0.0)

        return masked

    for d in range(2):
        previous = [None, None]
        for j in range(BLOCKS):
            parts = head_block(taps_ref[d, j], first_ref, second_ref, keep(j))
            for o in range(2):
                previous[o] = carried(class_window(parts, o, COLS), previous[o])
                sum_ref[d, o, STEP * j + 7 : STEP * j + 15, :] = previous[o]
        for o in range(2):
            shift = jnp.concatenate([shift_ref[o], shift_ref[o]], axis=1)
            for k in range(8):
                out_ref[d, o, 8 * k : 8 * k + 8, :] = sum_ref[d, o, 8 * k + 8 : 8 * k + 16, :] + shift


def edge_kernel(
    place_ref, window_ref, before_ref, after_ref, near_ref, first_ref, second_ref, shift_ref, done_ref,
    out_ref, taps_ref, sum_ref,
):
    lane = iota((ROWS, 128), 1)
    before, after = before_ref[...].astype(F32), after_ref[...].astype(F32)

    def pixels(slot, part):
        k = 2 * slot + part
        value = window_ref[slot, part].astype(F32)
        own_first = pltpu.roll(value[:, :128], EDGE, 1)
        own_last = pltpu.roll(value[:, 128:], 96, 1)
        left = pltpu.roll(before, 128 - EDGE * k, 1) if k else before
        right = pltpu.roll(after, 96 - EDGE * k, 1)
        tile = jnp.where(lane < EDGE, left, own_first)
        tile = jnp.where(lane < 64, tile, own_last)
        tile = jnp.where(lane < 96, tile, right)
        return jnp.where(lane < 112, tile, 0.0)

    planes = products([pixels(s, 0) for s in range(3)], [pixels(s, 1) for s in range(3)])
    source, target = iota((128, 128), 0), iota((128, 128), 1)
    from_col = jnp.where(source < 64, source - 16, source + 160)
    side = target % 64 // 32
    to_col = target % 32 + jnp.where(side == 0, -4, 232)
    gap = from_col - to_col + BOX_RG // 2
    near = (gap >= 0) & (gap < BOX_RG) & (source // 64 == side)
    bands = [(near & (target // 64 == d)).astype(BF16) for d in range(2)]
    band = jnp.concatenate([bands[0], bands[0], bands[1], bands[1]], axis=0)
    dates = [jnp.concatenate([planes[0]] + planes[1 + 4 * d : 5 + 4 * d], axis=0) for d in range(2)]
    summed = matmul(jnp.concatenate(halves(dates[0]) + halves(dates[1]), axis=1), band)

    def paired(value):
        return jnp.concatenate([value[:48], value[48:]], axis=1)

    boxed = [paired(sum_rows(summed[ROWS * k : ROWS * k + ROWS], near_ref)) for k in range(5)]
    place = place_ref[0]

    def in_frame(rows):
        spot = iota((rows, COLS), 1)
        column = spot % 32 + jnp.where(spot % 64 < 32, -4, 232)
        low = jnp.where(place == 0, 0, -128)
        high = jnp.where(place == place_ref[1] - 1, COLS, 2 * COLS)
        return (column >= low) & (column < high)

    valid = in_frame(48)
    base = jnp.where(iota((48, COLS), 1) < 128, 0, STEP * BLOCKS // 2 + 3)
    shared = mean_log(boxed[0], window_rows((48, COLS), base) & valid)
    store_shared(shared, [taps_ref], 128)
    taken = features(boxed[0], jnp.log(boxed[0] + EPSILON), boxed[1:])
    store_taps([jnp.where(valid, f, 0.0) for f in taken], taps_ref, 128)
    kept = in_frame(WIDE)
    row, spot = iota((WIDE, COLS), 0), iota((WIDE, COLS), 1)
    ended = kept & ((spot < 128) | (row < 4 * HIDDEN))
    sum_ref[...] = jnp.zeros_like(sum_ref)
    previous = [None, None]
    for j in range(6):
        masked = lambda hidden: jnp.where(ended if j == 4 else kept, hidden, 0.0)
        parts = head_block(taps_ref[j], first_ref, second_ref, masked)
        for o in range(2):
            previous[o] = carried(class_window(parts, o, 128), previous[o])
            at = STEP * j + 7
            sum_ref[o, at : at + 8, :128] = previous[o][:, :128]
            sum_ref[o, at + 36 : at + 44, 128:] = previous[o][:, 128:]
    spot = iota((8, 128), 1)
    for k in range(8):
        at, to = slice(8 * k + 8, 8 * k + 16), slice(8 * k, 8 * k + 8)
        for o in range(2):
            value = sum_ref[o, at, :128] + sum_ref[o, at, 128:] + shift_ref[o]
            for d in range(2):
                left = pltpu.roll(value, 128 - 64 * d - 4, 1)
                right = pltpu.roll(value, (112 - 64 * d - 40) % 128, 1)
                out_ref[d, o, to, :128] = jnp.where(spot < EDGE, left, done_ref[d, o, to, :128])
                out_ref[d, o, to, 128:] = jnp.where(spot >= 112, right, done_ref[d, o, to, 128:])


def vmem():
    return pl.BlockSpec(memory_space=pltpu.VMEM)


def smem():
    return pl.BlockSpec(memory_space=pltpu.SMEM)


def small(mib):
    return pltpu.CompilerParams(vmem_limit_bytes=mib << 20)


def local(
    slave_complex_pixels,
    along_track_line_groups,
    master_epoch_position,
    sweep_identifier,
    initial_filter_kernel,
    initial_filter_shift,
    latter_filter_kernel,
    latter_filter_shift,
):
    date_index = lax.axis_index("date")
    rng_count = lax.axis_size("rng")
    chosen = master_epoch_position[0]
    sent = pl.pallas_call(
        send_kernel,
        out_shape=jax.ShapeDtypeStruct((BANDS, 3, 2, 8, COLS), BF16),
        in_specs=[smem(), vmem()],
        out_specs=vmem(),
        compiler_params=small(4),
    )(master_epoch_position, slave_complex_pixels.reshape(BANDS, 2, 2, 8, COLS))
    bands = lax.all_to_all(sent, "date", split_axis=0, concat_axis=0, tiled=True)

    lists = along_track_line_groups[:, 0, :]
    mine = lax.dynamic_slice_in_dim(lists, date_index * 2, 2, 0)
    lists = jnp.concatenate([mine, lax.dynamic_slice_in_dim(lists, chosen, 1, 0)], axis=0)
    row_of = lax.broadcasted_iota(jnp.int32, (3, ROWS, 8 * BANDS), 2)
    picks = (lists[:, :, None] == row_of).astype(BF16)

    window = jnp.arange(8 * WINDOWS)
    frame_row = window // 8 * STEP - 1 + window % 8
    row_id = jnp.arange(ROWS)
    burst = sweep_identifier.astype(jnp.int32)
    target_burst = jnp.sum(jnp.where(frame_row[:, None] == row_id[None, :], burst[None, :], 0), axis=1)
    near = (
        (jnp.abs(row_id[None, :] - frame_row[:, None]) <= BOX_AZ // 2)
        & (burst[None, :] == target_burst[:, None])
        & (frame_row >= 0)[:, None]
        & (frame_row < ROWS)[:, None]
    ).astype(BF16)
    near = jnp.concatenate([near, near], axis=1)

    first = jnp.concatenate(
        [
            initial_filter_kernel.reshape(HIDDEN, 45),
            initial_filter_shift[:, None],
            jnp.zeros((HIDDEN, 2), F32),
        ],
        axis=1,
    )
    second = jnp.pad(
        jnp.transpose(latter_filter_kernel, (2, 3, 0, 1)).reshape(18, HIDDEN), ((0, 6), (0, 0))
    )
    first_spread, second_spread, shift = pl.pallas_call(
        spread_kernel,
        out_shape=(
            jax.ShapeDtypeStruct((2 * WIDE, COLS), BF16),
            jax.ShapeDtypeStruct((96, WIDE), BF16),
            jax.ShapeDtypeStruct((2, 8, 128), F32),
        ),
        in_specs=[vmem()] * 2 + [smem()],
        out_specs=(vmem(),) * 3,
        compiler_params=small(8),
        cost_estimate=pl.CostEstimate(flops=10**7, bytes_accessed=10**6, transcendentals=0),
    )(first, second, latter_filter_shift)

    pixels, first_edge, last_edge = pl.pallas_call(
        pick_kernel,
        out_shape=(
            jax.ShapeDtypeStruct((3, 2, ROWS, COLS), BF16),
            jax.ShapeDtypeStruct((ROWS, 128), BF16),
            jax.ShapeDtypeStruct((ROWS, 128), BF16),
        ),
        in_specs=[vmem()] * 2,
        out_specs=(vmem(),) * 3,
        compiler_params=small(8),
    )(picks, bands)

    up = [(i, i + 1) for i in range(rng_count - 1)]
    down = [(i + 1, i) for i in range(rng_count - 1)]
    before = lax.ppermute(last_edge, "rng", up)
    after = lax.ppermute(first_edge, "rng", down)

    middle = pl.pallas_call(
        middle_kernel,
        out_shape=jax.ShapeDtypeStruct((2, 2, ROWS, COLS), F32),
        in_specs=[vmem()] * 5,
        out_specs=vmem(),
        scratch_shapes=[
            pltpu.VMEM((2, BLOCKS, 256, COLS), BF16),
            pltpu.VMEM((2, 2, 80, COLS), F32),
        ],
        compiler_params=small(16),
        cost_estimate=pl.CostEstimate(flops=4 * 10**9, bytes_accessed=10**7, transcendentals=10**5),
    )(pixels, near, first_spread, second_spread, shift)

    place = jnp.stack([lax.axis_index("rng"), jnp.int32(rng_count)]).astype(jnp.int32)
    return pl.pallas_call(
        edge_kernel,
        out_shape=jax.ShapeDtypeStruct((2, 2, ROWS, COLS), F32),
        in_specs=[smem()] + [vmem()] * 8,
        out_specs=vmem(),
        scratch_shapes=[
            pltpu.VMEM((6, 256, COLS), BF16),
            pltpu.VMEM((2, 88, COLS), F32),
        ],
        compiler_params=small(16),
    )(place, pixels, before, after, near, first_spread, second_spread, shift, middle)


def solution(mesh):
    placed = (P(None, None, "date", "rng"), P(None, "rng", None), P(), P(), P(), P(), P(), P())
    return jax.shard_map(
        local, mesh=mesh, in_specs=placed, out_specs=P("date", None, None, "rng"), check_vma=False
    )
```

```python
import jax
import jax.numpy as jnp
from jax import lax
from jax.experimental import pallas as pl
from jax.experimental.pallas import tpu as pltpu
from jax.sharding import PartitionSpec as P

BOX_AZ = 7
BOX_RG = 28
EPSILON = 1e-06
ROWS = 64
COLS = 256
BANDS = 16
EDGE = 16
STEP = 6
BLOCKS = 11
WINDOWS = 12
HIDDEN = 32
WIDE = STEP * HIDDEN
F32 = jnp.float32
BF16 = jnp.bfloat16


def iota(shape, dim):
    return lax.broadcasted_iota(jnp.int32, shape, dim)


def halves(value):
    high = value.astype(BF16)
    return high, (value - high.astype(F32)).astype(BF16)


def matmul(left, right):
    return jnp.dot(left, right, preferred_element_type=F32)


def send_kernel(chosen_ref, own_ref, sent_ref):
    chosen = chosen_ref[0]
    sent_ref[:, :2] = own_ref[...]
    master = own_ref[chosen // 2, chosen % 2]
    for band in range(BANDS):
        sent_ref[band, 2] = master


def spread_kernel(first_ref, second_ref, shift_ref, first_out, second_out, shift_out):
    row, col = iota((WIDE, 128), 0), iota((WIDE, 128), 1)
    tap = col % 8 - row // HIDDEN
    widen = (iota((WIDE, HIDDEN), 0) % HIDDEN == iota((WIDE, HIDDEN), 1)).astype(BF16)
    source, target = iota((48, 128), 0), iota((48, 128), 1)
    piece = target // 8
    shift = jnp.where(piece < 6, piece // 2, jnp.where(piece < 12, piece // 2 - 3, piece - 12))
    feature = jnp.where(piece < 6, piece % 2, jnp.where(piece < 12, 2 + piece % 2, 4))
    base = feature * 9 + shift
    offset = ((source == 45) & (target == 120)).astype(BF16)
    taken = [((source == base + 3 * a) & (piece < 15)).astype(BF16) for a in range(3)]
    for part, half in enumerate(halves(first_ref[...])):
        tall = matmul(widen, half).astype(BF16)
        spread = jnp.zeros((WIDE, 128), F32)
        for a in range(3):
            spread = jnp.where(tap == a, matmul(tall, taken[a]), spread)
        at = slice(WIDE * part, WIDE * part + WIDE)
        first_out[at, :128] = (spread + matmul(tall, offset)).astype(BF16)
        first_out[at, 128:] = (spread if part == 0 else jnp.zeros_like(spread)).astype(BF16)
    row, col = iota((48, WIDE), 0), iota((48, WIDE), 1)
    tap = col // HIDDEN + 2 - row % 8
    widen = (iota((HIDDEN, WIDE), 1) % HIDDEN == iota((HIDDEN, WIDE), 0)).astype(BF16)
    group, source = iota((48, 24), 0) // 8, iota((48, 24), 1)
    for part, half in enumerate(halves(second_ref[...])):
        wide = matmul(half, widen).astype(BF16)
        spread = jnp.zeros((48, WIDE), F32)
        for a in range(3):
            chosen = (source == group + 6 * a).astype(BF16)
            spread = jnp.where(tap == a, matmul(chosen, wide), spread)
        second_out[48 * part : 48 * part + 48, :] = spread.astype(BF16)
    for o in range(2):
        shift_out[o] = jnp.full((8, 128), shift_ref[o], F32)


def pick_kernel(chosen_ref, bands_ref, window_ref, first_ref, last_ref):
    lane = iota((ROWS, 128), 1)
    first = jnp.zeros((ROWS, 128), F32)
    last = jnp.zeros((ROWS, 128), F32)
    for slot in range(3):
        for part in range(2):
            k = 2 * slot + part
            rows = bands_ref[:, slot, part].astype(F32).reshape(8 * BANDS, COLS).astype(BF16)
            picked = matmul(chosen_ref[slot], rows)
            window_ref[slot, part] = picked.astype(BF16)
            here = (lane >= EDGE * k) & (lane < EDGE * (k + 1))
            left = picked[:, :128]
            right = pltpu.roll(picked[:, 128:], EDGE * (k + 1), 1)
            if k:
                left = pltpu.roll(left, EDGE * k, 1)
            first = jnp.where(here, left, first)
            last = jnp.where(here, right, last)
    first_ref[...] = first.astype(BF16)
    last_ref[...] = last.astype(BF16)


def products(re, im):
    ref_re, ref_im = re[2], im[2]
    pow_ref = ref_re * ref_re + ref_im * ref_im
    planes = [pow_ref]
    for d in range(2):
        pow_sec = re[d] * re[d] + im[d] * im[d]
        planes += [
            pow_sec,
            ref_re * re[d] + ref_im * im[d],
            ref_im * re[d] - ref_re * im[d],
            jnp.sqrt(pow_ref * pow_sec),
        ]
    return planes


def sum_rows(summed, near_ref):
    return matmul(near_ref[...], jnp.concatenate(halves(summed), axis=0))


def mean_log(box_ref, inside):
    return jnp.where(inside, jnp.log(box_ref / (BOX_AZ * BOX_RG) + EPSILON), 0.0)


def features(box_ref, log_ref, boxed):
    inverse = 1.0 / (jnp.sqrt(box_ref * boxed[0]) + EPSILON)
    ratio = jnp.log(boxed[0] + EPSILON) - log_ref
    return boxed[1] * inverse, boxed[2] * inverse, boxed[3] * inverse, ratio


def window_rows(rows, base):
    row = iota(rows, 0)
    frame_row = row // 8 * STEP - 1 + row % 8 + base
    return (frame_row >= 0) & (frame_row < ROWS)


def sideways(value, b, span):
    if b == 1:
        return value
    width = value.shape[1]
    if span == width:
        return pltpu.roll(value, 1 if b == 0 else width - 1, 1)
    pieces = [sideways(value[:, at : at + span], b, span) for at in range(0, width, span)]
    return jnp.concatenate(pieces, axis=1)


def store_pieces(taps_ref, piece, upper, lower):
    for j in range(taps_ref.shape[0]):
        at = slice(8 * j, 8 * j + 8)
        high, low = halves(jnp.concatenate([upper[at], lower[at]], axis=0))
        taps_ref[j, 8 * piece : 8 * piece + 16, :] = high
        taps_ref[j, 128 + 8 * piece : 144 + 8 * piece, :] = low


def store_taps(taken, taps_ref, span):
    for pair in range(2):
        for b in range(3):
            upper, lower = [sideways(taken[2 * pair + k], b, span) for k in range(2)]
            store_pieces(taps_ref, 6 * pair + 2 * b, upper, lower)


def store_shared(shared, taps_refs, span):
    moved = [sideways(shared, b, span) for b in range(3)]
    one = jnp.where(iota(shared.shape, 0) % 8 == 0, 1.0, 0.0)
    for taps_ref in taps_refs:
        store_pieces(taps_ref, 12, moved[0], moved[1])
        store_pieces(taps_ref, 14, moved[2], one)


def first_part(taps, first_ref):
    doubled = matmul(first_ref[...], taps)
    return doubled[:WIDE] + doubled[WIDE:]


def second_part(sums, second_ref, keep):
    high, low = halves(keep(jnp.maximum(sums, 0.0)))
    doubled = matmul(second_ref[...], high)
    return doubled[:48] + doubled[48:] + matmul(second_ref[:48, :], low)


def class_window(parts, o, span):
    groups = [parts[16 * b + 8 * o : 16 * b + 8 * o + 8] for b in range(3)]
    return sum(sideways(groups[b], b, span) for b in range(3))


def carried(window, previous):
    if previous is None:
        return window
    row = iota(window.shape, 0)
    return window + jnp.where(row < 2, pltpu.roll(previous, 2, 0), 0.0)


def middle_kernel(window_ref, near_ref, first_ref, second_ref, shift_ref, out_ref, taps_ref, sum_ref):
    re = [window_ref[s, 0].astype(F32) for s in range(3)]
    im = [window_ref[s, 1].astype(F32) for s in range(3)]
    gap = iota((COLS, COLS), 0) - iota((COLS, COLS), 1) + BOX_RG // 2
    band = ((gap >= 0) & (gap < BOX_RG)).astype(BF16)
    planes = jnp.concatenate(products(re, im), axis=0)
    summed = matmul(jnp.concatenate(halves(planes), axis=1), jnp.concatenate([band, band], axis=0))
    live = 8 * BLOCKS
    boxed = [sum_rows(summed[ROWS * k : ROWS * k + ROWS], near_ref)[:live] for k in range(9)]
    log_ref = jnp.log(boxed[0] + EPSILON)
    shared = mean_log(boxed[0], window_rows((live, COLS), 0))
    sides = [taps_ref.at[:, :, COLS * d : COLS * d + COLS] for d in range(2)]
    store_shared(shared, sides, COLS)
    for d in range(2):
        store_taps(features(boxed[0], log_ref, boxed[1 + 4 * d : 5 + 4 * d]), sides[d], COLS)

    def keep(j):
        def masked(hidden):
            if j < BLOCKS - 1:
                return hidden
            row = iota(hidden.shape, 0)
            return jnp.where(row < (ROWS - STEP * j) * HIDDEN, hidden, 0.0)

        return masked

    previous = [None, None]
    ahead = first_part(taps_ref[0], first_ref)
    for j in range(BLOCKS):
        later = first_part(taps_ref[j + 1], first_ref) if j + 1 < BLOCKS else None
        parts = second_part(ahead, second_ref, keep(j))
        ahead = later
        for o in range(2):
            previous[o] = carried(class_window(parts, o, COLS), previous[o])
            sum_ref[o, STEP * j + 7 : STEP * j + 15, :] = previous[o]
    for d in range(2):
        for o in range(2):
            shift = jnp.concatenate([shift_ref[o], shift_ref[o]], axis=1)
            for k in range(8):
                done = sum_ref[o, 8 * k + 8 : 8 * k + 16, COLS * d : COLS * d + COLS]
                out_ref[d, o, 8 * k : 8 * k + 8, :] = done + shift


def edge_kernel(
    place_ref, window_ref, before_ref, after_ref, near_ref, first_ref, second_ref, shift_ref, done_ref,
    out_ref, taps_ref, sum_ref,
):
    lane = iota((ROWS, 128), 1)
    place = place_ref[0]
    before = jnp.where(place == 0, 0.0, before_ref[...].astype(F32))
    after = jnp.where(place == place_ref[1] - 1, 0.0, after_ref[...].astype(F32))

    def pixels(slot, part):
        k = 2 * slot + part
        value = window_ref[slot, part].astype(F32)
        own_first = pltpu.roll(value[:, :128], EDGE, 1)
        own_last = pltpu.roll(value[:, 128:], 96, 1)
        left = pltpu.roll(before, 128 - EDGE * k, 1) if k else before
        right = pltpu.roll(after, 96 - EDGE * k, 1)
        tile = jnp.where(lane < EDGE, left, own_first)
        tile = jnp.where(lane < 64, tile, own_last)
        tile = jnp.where(lane < 96, tile, right)
        return jnp.where(lane < 112, tile, 0.0)

    planes = products([pixels(s, 0) for s in range(3)], [pixels(s, 1) for s in range(3)])
    source, target = iota((128, 128), 0), iota((128, 128), 1)
    from_col = jnp.where(source < 64, source - 16, source + 160)
    side = target % 64 // 32
    to_col = target % 32 + jnp.where(side == 0, -4, 232)
    gap = from_col - to_col + BOX_RG // 2
    near = (gap >= 0) & (gap < BOX_RG) & (source // 64 == side)
    bands = [(near & (target // 64 == d)).astype(BF16) for d in range(2)]
    band = jnp.concatenate([bands[0], bands[0], bands[1], bands[1]], axis=0)
    dates = [jnp.concatenate([planes[0]] + planes[1 + 4 * d : 5 + 4 * d], axis=0) for d in range(2)]
    summed = matmul(jnp.concatenate(halves(dates[0]) + halves(dates[1]), axis=1), band)

    def spread(value):
        return jnp.concatenate([value[24 * q : 24 * q + 24] for q in range(4)], axis=1)

    boxed = [spread(sum_rows(summed[ROWS * k : ROWS * k + ROWS], near_ref)) for k in range(5)]

    def in_frame(rows):
        spot = iota((rows, 512), 1)
        column = spot % 32 + jnp.where(spot % 64 < 32, -4, 232)
        low = jnp.where(place == 0, 0, -128)
        high = jnp.where(place == place_ref[1] - 1, COLS, 2 * COLS)
        return (column >= low) & (column < high)

    valid = in_frame(24)
    base = iota((24, 512), 1) // 128 * (3 * STEP)
    shared = mean_log(boxed[0], window_rows((24, 512), base) & valid)
    store_shared(shared, [taps_ref], 128)
    taken = features(boxed[0], jnp.log(boxed[0] + EPSILON), boxed[1:])
    store_taps([jnp.where(valid, f, 0.0) for f in taken], taps_ref, 128)
    kept = in_frame(WIDE)
    row, spot = iota((WIDE, 512), 0), iota((WIDE, 512), 1)
    ended = kept & ((spot < 384) | (row < 4 * HIDDEN))
    sum_ref[...] = jnp.zeros_like(sum_ref)
    previous = [None, None]
    ahead = first_part(taps_ref[0], first_ref)
    for j in range(3):
        later = first_part(taps_ref[j + 1], first_ref) if j < 2 else None
        mask = ended if j == 1 else kept
        parts = second_part(ahead, second_ref, lambda hidden: jnp.where(mask, hidden, 0.0))
        ahead = later
        for o in range(2):
            previous[o] = carried(class_window(parts, o, 128), previous[o])
            for q in range(4):
                at, lanes = STEP * (j + 3 * q) + 7, slice(128 * q, 128 * q + 128)
                sum_ref[o, at : at + 8, lanes] = previous[o][:, lanes]
    spot = iota((8, 128), 1)
    for k in range(8):
        at, to = slice(8 * k + 8, 8 * k + 16), slice(8 * k, 8 * k + 8)
        for o in range(2):
            value = sum(sum_ref[o, at, 128 * q : 128 * q + 128] for q in range(4)) + shift_ref[o]
            for d in range(2):
                left = pltpu.roll(value, 128 - 64 * d - 4, 1)
                right = pltpu.roll(value, (112 - 64 * d - 40) % 128, 1)
                out_ref[d, o, to, :128] = jnp.where(spot < EDGE, left, done_ref[d, o, to, :128])
                out_ref[d, o, to, 128:] = jnp.where(spot >= 112, right, done_ref[d, o, to, 128:])


def vmem():
    return pl.BlockSpec(memory_space=pltpu.VMEM)


def smem():
    return pl.BlockSpec(memory_space=pltpu.SMEM)


def small(mib):
    return pltpu.CompilerParams(vmem_limit_bytes=mib << 20)


def local(
    slave_complex_pixels,
    along_track_line_groups,
    master_epoch_position,
    sweep_identifier,
    initial_filter_kernel,
    initial_filter_shift,
    latter_filter_kernel,
    latter_filter_shift,
):
    date_index = lax.axis_index("date")
    rng_count = lax.axis_size("rng")
    chosen = master_epoch_position[0]
    sent = pl.pallas_call(
        send_kernel,
        out_shape=jax.ShapeDtypeStruct((BANDS, 3, 2, 8, COLS), BF16),
        in_specs=[smem(), vmem()],
        out_specs=vmem(),
        compiler_params=small(4),
    )(master_epoch_position, slave_complex_pixels.reshape(BANDS, 2, 2, 8, COLS))
    bands = lax.all_to_all(sent, "date", split_axis=0, concat_axis=0, tiled=True)

    lists = along_track_line_groups[:, 0, :]
    mine = lax.dynamic_slice_in_dim(lists, date_index * 2, 2, 0)
    lists = jnp.concatenate([mine, lax.dynamic_slice_in_dim(lists, chosen, 1, 0)], axis=0)
    row_of = lax.broadcasted_iota(jnp.int32, (3, ROWS, 8 * BANDS), 2)
    picks = (lists[:, :, None] == row_of).astype(BF16)

    window = jnp.arange(8 * WINDOWS)
    frame_row = window // 8 * STEP - 1 + window % 8
    row_id = jnp.arange(ROWS)
    burst = sweep_identifier.astype(jnp.int32)
    target_burst = jnp.sum(jnp.where(frame_row[:, None] == row_id[None, :], burst[None, :], 0), axis=1)
    near = (
        (jnp.abs(row_id[None, :] - frame_row[:, None]) <= BOX_AZ // 2)
        & (burst[None, :] == target_burst[:, None])
        & (frame_row >= 0)[:, None]
        & (frame_row < ROWS)[:, None]
    ).astype(BF16)
    near = jnp.concatenate([near, near], axis=1)

    first = jnp.concatenate(
        [
            initial_filter_kernel.reshape(HIDDEN, 45),
            initial_filter_shift[:, None],
            jnp.zeros((HIDDEN, 2), F32),
        ],
        axis=1,
    )
    second = jnp.pad(
        jnp.transpose(latter_filter_kernel, (2, 3, 0, 1)).reshape(18, HIDDEN), ((0, 6), (0, 0))
    )
    first_spread, second_spread, shift = pl.pallas_call(
        spread_kernel,
        out_shape=(
            jax.ShapeDtypeStruct((2 * WIDE, COLS), BF16),
            jax.ShapeDtypeStruct((96, WIDE), BF16),
            jax.ShapeDtypeStruct((2, 8, 128), F32),
        ),
        in_specs=[vmem()] * 2 + [smem()],
        out_specs=(vmem(),) * 3,
        compiler_params=small(8),
        cost_estimate=pl.CostEstimate(flops=10**7, bytes_accessed=10**6, transcendentals=0),
    )(first, second, latter_filter_shift)

    pixels, first_edge, last_edge = pl.pallas_call(
        pick_kernel,
        out_shape=(
            jax.ShapeDtypeStruct((3, 2, ROWS, COLS), BF16),
            jax.ShapeDtypeStruct((ROWS, 128), BF16),
            jax.ShapeDtypeStruct((ROWS, 128), BF16),
        ),
        in_specs=[vmem()] * 2,
        out_specs=(vmem(),) * 3,
        compiler_params=small(8),
    )(picks, bands)

    up = [(i, (i + 1) % rng_count) for i in range(rng_count)]
    down = [(j, i) for i, j in up]
    before = lax.ppermute(last_edge, "rng", up)
    after = lax.ppermute(first_edge, "rng", down)

    middle = pl.pallas_call(
        middle_kernel,
        out_shape=jax.ShapeDtypeStruct((2, 2, ROWS, COLS), F32),
        in_specs=[vmem()] * 5,
        out_specs=vmem(),
        scratch_shapes=[
            pltpu.VMEM((BLOCKS, 256, 2 * COLS), BF16),
            pltpu.VMEM((2, 80, 2 * COLS), F32),
        ],
        compiler_params=small(16),
        cost_estimate=pl.CostEstimate(flops=4 * 10**9, bytes_accessed=10**7, transcendentals=10**5),
    )(pixels, near, first_spread, second_spread, shift)

    place = jnp.stack([lax.axis_index("rng"), jnp.int32(rng_count)]).astype(jnp.int32)
    return pl.pallas_call(
        edge_kernel,
        out_shape=jax.ShapeDtypeStruct((2, 2, ROWS, COLS), F32),
        in_specs=[smem()] + [vmem()] * 8,
        out_specs=vmem(),
        scratch_shapes=[
            pltpu.VMEM((3, 256, 512), BF16),
            pltpu.VMEM((2, 88, 512), F32),
        ],
        compiler_params=small(16),
    )(place, pixels, before, after, near, first_spread, second_spread, shift, middle)


def solution(mesh):
    placed = (P(None, None, "date", "rng"), P(None, "rng", None), P(), P(), P(), P(), P(), P())
    return jax.shard_map(
        local, mesh=mesh, in_specs=placed, out_specs=P("date", None, None, "rng"), check_vma=False
    )
```

```python
import jax
import jax.numpy as jnp
from jax import lax
from jax.experimental import pallas as pl
from jax.experimental.pallas import tpu as pltpu
from jax.sharding import PartitionSpec as P

BOX_AZ = 7
BOX_RG = 28
EPSILON = 1e-06
ROWS = 64
COLS = 256
BANDS = 16
EDGE = 16
STEP = 6
BLOCKS = 11
WINDOWS = 12
HIDDEN = 32
WIDE = STEP * HIDDEN
F32 = jnp.float32
BF16 = jnp.bfloat16


def iota(shape, dim):
    return lax.broadcasted_iota(jnp.int32, shape, dim)


def halves(value):
    high = value.astype(BF16)
    return high, (value - high.astype(F32)).astype(BF16)


def matmul(left, right):
    return jnp.dot(left, right, preferred_element_type=F32)


def send_kernel(chosen_ref, own_ref, sent_ref):
    chosen = chosen_ref[0]
    sent_ref[:, :2] = own_ref[...]
    master = own_ref[chosen // 2, chosen % 2]
    for band in range(BANDS):
        sent_ref[band, 2] = master


def spread_kernel(first_ref, second_ref, shift_ref, first_out, second_out, shift_out):
    row, col = iota((WIDE, 128), 0), iota((WIDE, 128), 1)
    tap = col % 8 - row // HIDDEN
    widen = (iota((WIDE, HIDDEN), 0) % HIDDEN == iota((WIDE, HIDDEN), 1)).astype(BF16)
    source, target = iota((48, 128), 0), iota((48, 128), 1)
    piece = target // 8
    shift = jnp.where(piece < 6, piece // 2, jnp.where(piece < 12, piece // 2 - 3, piece - 12))
    feature = jnp.where(piece < 6, piece % 2, jnp.where(piece < 12, 2 + piece % 2, 4))
    base = feature * 9 + shift
    offset = ((source == 45) & (target == 120)).astype(BF16)
    taken = [((source == base + 3 * a) & (piece < 15)).astype(BF16) for a in range(3)]
    for part, half in enumerate(halves(first_ref[...])):
        tall = matmul(widen, half).astype(BF16)
        spread = jnp.zeros((WIDE, 128), F32)
        for a in range(3):
            spread = jnp.where(tap == a, matmul(tall, taken[a]), spread)
        at = slice(WIDE * part, WIDE * part + WIDE)
        first_out[at, :128] = (spread + matmul(tall, offset)).astype(BF16)
        first_out[at, 128:] = (spread if part == 0 else jnp.zeros_like(spread)).astype(BF16)
    row, col = iota((48, WIDE), 0), iota((48, WIDE), 1)
    tap = col // HIDDEN + 2 - row % 8
    widen = (iota((HIDDEN, WIDE), 1) % HIDDEN == iota((HIDDEN, WIDE), 0)).astype(BF16)
    group, source = iota((48, 24), 0) // 8, iota((48, 24), 1)
    for part, half in enumerate(halves(second_ref[...])):
        wide = matmul(half, widen).astype(BF16)
        spread = jnp.zeros((48, WIDE), F32)
        for a in range(3):
            chosen = (source == group + 6 * a).astype(BF16)
            spread = jnp.where(tap == a, matmul(chosen, wide), spread)
        second_out[48 * part : 48 * part + 48, :] = spread.astype(BF16)
    for o in range(2):
        shift_out[o] = jnp.full((8, 128), shift_ref[o], F32)


def pick_kernel(chosen_ref, bands_ref, window_ref, inner_ref, outer_ref):
    odd = lax.axis_index("rng") % 2 == 1
    lane = iota((ROWS, 128), 1)
    first = jnp.zeros((ROWS, 128), F32)
    last = jnp.zeros((ROWS, 128), F32)
    for slot in range(3):
        for part in range(2):
            k = 2 * slot + part
            rows = bands_ref[:, slot, part].astype(F32).reshape(8 * BANDS, COLS).astype(BF16)
            picked = matmul(chosen_ref[slot], rows)
            window_ref[slot, part] = picked.astype(BF16)
            here = (lane >= EDGE * k) & (lane < EDGE * (k + 1))
            left = picked[:, :128]
            right = pltpu.roll(picked[:, 128:], EDGE * (k + 1), 1)
            if k:
                left = pltpu.roll(left, EDGE * k, 1)
            first = jnp.where(here, left, first)
            last = jnp.where(here, right, last)
    inner_ref[...] = jnp.where(odd, first, last).astype(BF16)
    outer_ref[...] = jnp.where(odd, last, first).astype(BF16)


def products(re, im):
    ref_re, ref_im = re[2], im[2]
    pow_ref = ref_re * ref_re + ref_im * ref_im
    planes = [pow_ref]
    for d in range(2):
        pow_sec = re[d] * re[d] + im[d] * im[d]
        planes += [
            pow_sec,
            ref_re * re[d] + ref_im * im[d],
            ref_im * re[d] - ref_re * im[d],
            jnp.sqrt(pow_ref * pow_sec),
        ]
    return planes


def sum_rows(summed, near_ref):
    return matmul(near_ref[...], jnp.concatenate(halves(summed), axis=0))


def mean_log(box_ref, inside):
    return jnp.where(inside, jnp.log(box_ref / (BOX_AZ * BOX_RG) + EPSILON), 0.0)


def features(box_ref, log_ref, boxed):
    inverse = 1.0 / (jnp.sqrt(box_ref * boxed[0]) + EPSILON)
    ratio = jnp.log(boxed[0] + EPSILON) - log_ref
    return boxed[1] * inverse, boxed[2] * inverse, boxed[3] * inverse, ratio


def window_rows(rows, base):
    row = iota(rows, 0)
    frame_row = row // 8 * STEP - 1 + row % 8 + base
    return (frame_row >= 0) & (frame_row < ROWS)


def sideways(value, b, span):
    if b == 1:
        return value
    width = value.shape[1]
    if span == width:
        return pltpu.roll(value, 1 if b == 0 else width - 1, 1)
    pieces = [sideways(value[:, at : at + span], b, span) for at in range(0, width, span)]
    return jnp.concatenate(pieces, axis=1)


def store_pieces(taps_ref, piece, upper, lower):
    for j in range(taps_ref.shape[0]):
        at = slice(8 * j, 8 * j + 8)
        high, low = halves(jnp.concatenate([upper[at], lower[at]], axis=0))
        taps_ref[j, 8 * piece : 8 * piece + 16, :] = high
        taps_ref[j, 128 + 8 * piece : 144 + 8 * piece, :] = low


def store_taps(taken, taps_ref, span):
    for pair in range(2):
        for b in range(3):
            upper, lower = [sideways(taken[2 * pair + k], b, span) for k in range(2)]
            store_pieces(taps_ref, 6 * pair + 2 * b, upper, lower)


def store_shared(shared, taps_refs, span):
    moved = [sideways(shared, b, span) for b in range(3)]
    one = jnp.where(iota(shared.shape, 0) % 8 == 0, 1.0, 0.0)
    for taps_ref in taps_refs:
        store_pieces(taps_ref, 12, moved[0], moved[1])
        store_pieces(taps_ref, 14, moved[2], one)


def first_part(taps, first_ref):
    doubled = matmul(first_ref[...], taps)
    return doubled[:WIDE] + doubled[WIDE:]


def second_part(sums, second_ref, keep):
    high, low = halves(keep(jnp.maximum(sums, 0.0)))
    doubled = matmul(second_ref[...], high)
    return doubled[:48] + doubled[48:] + matmul(second_ref[:48, :], low)


def class_window(parts, o, span):
    groups = [parts[16 * b + 8 * o : 16 * b + 8 * o + 8] for b in range(3)]
    return sum(sideways(groups[b], b, span) for b in range(3))


def carried(window, previous):
    if previous is None:
        return window
    row = iota(window.shape, 0)
    return window + jnp.where(row < 2, pltpu.roll(previous, 2, 0), 0.0)


def middle_kernel(window_ref, near_ref, first_ref, second_ref, shift_ref, out_ref, taps_ref, sum_ref):
    re = [window_ref[s, 0].astype(F32) for s in range(3)]
    im = [window_ref[s, 1].astype(F32) for s in range(3)]
    gap = iota((COLS, COLS), 0) - iota((COLS, COLS), 1) + BOX_RG // 2
    band = ((gap >= 0) & (gap < BOX_RG)).astype(BF16)
    planes = jnp.concatenate(products(re, im), axis=0)
    summed = matmul(jnp.concatenate(halves(planes), axis=1), jnp.concatenate([band, band], axis=0))
    live = 8 * BLOCKS
    boxed = [sum_rows(summed[ROWS * k : ROWS * k + ROWS], near_ref)[:live] for k in range(9)]
    log_ref = jnp.log(boxed[0] + EPSILON)
    shared = mean_log(boxed[0], window_rows((live, COLS), 0))
    sides = [taps_ref.at[:, :, COLS * d : COLS * d + COLS] for d in range(2)]
    store_shared(shared, sides, COLS)
    for d in range(2):
        store_taps(features(boxed[0], log_ref, boxed[1 + 4 * d : 5 + 4 * d]), sides[d], COLS)

    def keep(j):
        def masked(hidden):
            if j < BLOCKS - 1:
                return hidden
            row = iota(hidden.shape, 0)
            return jnp.where(row < (ROWS - STEP * j) * HIDDEN, hidden, 0.0)

        return masked

    previous = [None, None]
    ahead = first_part(taps_ref[0], first_ref)
    for j in range(BLOCKS):
        later = first_part(taps_ref[j + 1], first_ref) if j + 1 < BLOCKS else None
        parts = second_part(ahead, second_ref, keep(j))
        ahead = later
        for o in range(2):
            previous[o] = carried(class_window(parts, o, COLS), previous[o])
            sum_ref[o, STEP * j + 7 : STEP * j + 15, :] = previous[o]
    for d in range(2):
        for o in range(2):
            shift = jnp.concatenate([shift_ref[o], shift_ref[o]], axis=1)
            for k in range(8):
                done = sum_ref[o, 8 * k + 8 : 8 * k + 16, COLS * d : COLS * d + COLS]
                out_ref[d, o, 8 * k : 8 * k + 8, :] = done + shift


def edge_kernel(
    window_ref, inner_ref, outer_ref, near_ref, first_ref, second_ref, shift_ref, done_ref,
    out_ref, taps_ref, sum_ref,
):
    lane = iota((ROWS, 128), 1)
    place, places = lax.axis_index("rng"), lax.axis_size("rng")
    odd = place % 2 == 1
    inner, outer = inner_ref[...].astype(F32), outer_ref[...].astype(F32)
    before = jnp.where(place == 0, 0.0, jnp.where(odd, inner, outer))
    after = jnp.where(place == places - 1, 0.0, jnp.where(odd, outer, inner))

    def pixels(slot, part):
        k = 2 * slot + part
        value = window_ref[slot, part].astype(F32)
        own_first = pltpu.roll(value[:, :128], EDGE, 1)
        own_last = pltpu.roll(value[:, 128:], 96, 1)
        left = pltpu.roll(before, 128 - EDGE * k, 1) if k else before
        right = pltpu.roll(after, 96 - EDGE * k, 1)
        tile = jnp.where(lane < EDGE, left, own_first)
        tile = jnp.where(lane < 64, tile, own_last)
        tile = jnp.where(lane < 96, tile, right)
        return jnp.where(lane < 112, tile, 0.0)

    planes = products([pixels(s, 0) for s in range(3)], [pixels(s, 1) for s in range(3)])
    source, target = iota((128, 128), 0), iota((128, 128), 1)
    from_col = jnp.where(source < 64, source - 16, source + 160)
    side = target % 64 // 32
    to_col = target % 32 + jnp.where(side == 0, -4, 232)
    gap = from_col - to_col + BOX_RG // 2
    near = (gap >= 0) & (gap < BOX_RG) & (source // 64 == side)
    bands = [(near & (target // 64 == d)).astype(BF16) for d in range(2)]
    band = jnp.concatenate([bands[0], bands[0], bands[1], bands[1]], axis=0)
    dates = [jnp.concatenate([planes[0]] + planes[1 + 4 * d : 5 + 4 * d], axis=0) for d in range(2)]
    summed = matmul(jnp.concatenate(halves(dates[0]) + halves(dates[1]), axis=1), band)

    def spread(value):
        return jnp.concatenate([value[24 * q : 24 * q + 24] for q in range(4)], axis=1)

    boxed = [spread(sum_rows(summed[ROWS * k : ROWS * k + ROWS], near_ref)) for k in range(5)]

    def in_frame(rows):
        spot = iota((rows, 512), 1)
        column = spot % 32 + jnp.where(spot % 64 < 32, -4, 232)
        low = jnp.where(place == 0, 0, -128)
        high = jnp.where(place == places - 1, COLS, 2 * COLS)
        return (column >= low) & (column < high)

    valid = in_frame(24)
    base = iota((24, 512), 1) // 128 * (3 * STEP)
    shared = mean_log(boxed[0], window_rows((24, 512), base) & valid)
    store_shared(shared, [taps_ref], 128)
    taken = features(boxed[0], jnp.log(boxed[0] + EPSILON), boxed[1:])
    store_taps([jnp.where(valid, f, 0.0) for f in taken], taps_ref, 128)
    kept = in_frame(WIDE)
    row, spot = iota((WIDE, 512), 0), iota((WIDE, 512), 1)
    ended = kept & ((spot < 384) | (row < 4 * HIDDEN))
    sum_ref[...] = jnp.zeros_like(sum_ref)
    previous = [None, None]
    ahead = first_part(taps_ref[0], first_ref)
    for j in range(3):
        later = first_part(taps_ref[j + 1], first_ref) if j < 2 else None
        mask = ended if j == 1 else kept
        parts = second_part(ahead, second_ref, lambda hidden: jnp.where(mask, hidden, 0.0))
        ahead = later
        for o in range(2):
            previous[o] = carried(class_window(parts, o, 128), previous[o])
            for q in range(4):
                at, lanes = STEP * (j + 3 * q) + 7, slice(128 * q, 128 * q + 128)
                sum_ref[o, at : at + 8, lanes] = previous[o][:, lanes]
    spot = iota((8, 128), 1)
    for k in range(8):
        at, to = slice(8 * k + 8, 8 * k + 16), slice(8 * k, 8 * k + 8)
        for o in range(2):
            value = sum(sum_ref[o, at, 128 * q : 128 * q + 128] for q in range(4)) + shift_ref[o]
            for d in range(2):
                left = pltpu.roll(value, 128 - 64 * d - 4, 1)
                right = pltpu.roll(value, (112 - 64 * d - 40) % 128, 1)
                out_ref[d, o, to, :128] = jnp.where(spot < EDGE, left, done_ref[d, o, to, :128])
                out_ref[d, o, to, 128:] = jnp.where(spot >= 112, right, done_ref[d, o, to, 128:])


def vmem():
    return pl.BlockSpec(memory_space=pltpu.VMEM)


def smem():
    return pl.BlockSpec(memory_space=pltpu.SMEM)


def small(mib):
    return pltpu.CompilerParams(vmem_limit_bytes=mib << 20)


def local(
    slave_complex_pixels,
    along_track_line_groups,
    master_epoch_position,
    sweep_identifier,
    initial_filter_kernel,
    initial_filter_shift,
    latter_filter_kernel,
    latter_filter_shift,
):
    date_index = lax.axis_index("date")
    rng_count = lax.axis_size("rng")
    chosen = master_epoch_position[0]
    sent = pl.pallas_call(
        send_kernel,
        out_shape=jax.ShapeDtypeStruct((BANDS, 3, 2, 8, COLS), BF16),
        in_specs=[smem(), vmem()],
        out_specs=vmem(),
        compiler_params=small(4),
    )(master_epoch_position, slave_complex_pixels.reshape(BANDS, 2, 2, 8, COLS))
    bands = lax.all_to_all(sent, "date", split_axis=0, concat_axis=0, tiled=True)

    lists = along_track_line_groups[:, 0, :]
    mine = lax.dynamic_slice_in_dim(lists, date_index * 2, 2, 0)
    lists = jnp.concatenate([mine, lax.dynamic_slice_in_dim(lists, chosen, 1, 0)], axis=0)
    row_of = lax.broadcasted_iota(jnp.int32, (3, ROWS, 8 * BANDS), 2)
    picks = (lists[:, :, None] == row_of).astype(BF16)

    window = jnp.arange(8 * WINDOWS)
    frame_row = window // 8 * STEP - 1 + window % 8
    row_id = jnp.arange(ROWS)
    burst = sweep_identifier.astype(jnp.int32)
    target_burst = jnp.sum(jnp.where(frame_row[:, None] == row_id[None, :], burst[None, :], 0), axis=1)
    near = (
        (jnp.abs(row_id[None, :] - frame_row[:, None]) <= BOX_AZ // 2)
        & (burst[None, :] == target_burst[:, None])
        & (frame_row >= 0)[:, None]
        & (frame_row < ROWS)[:, None]
    ).astype(BF16)
    near = jnp.concatenate([near, near], axis=1)

    first = jnp.concatenate(
        [
            initial_filter_kernel.reshape(HIDDEN, 45),
            initial_filter_shift[:, None],
            jnp.zeros((HIDDEN, 2), F32),
        ],
        axis=1,
    )
    second = jnp.pad(
        jnp.transpose(latter_filter_kernel, (2, 3, 0, 1)).reshape(18, HIDDEN), ((0, 6), (0, 0))
    )
    first_spread, second_spread, shift = pl.pallas_call(
        spread_kernel,
        out_shape=(
            jax.ShapeDtypeStruct((2 * WIDE, COLS), BF16),
            jax.ShapeDtypeStruct((96, WIDE), BF16),
            jax.ShapeDtypeStruct((2, 8, 128), F32),
        ),
        in_specs=[vmem()] * 2 + [smem()],
        out_specs=(vmem(),) * 3,
        compiler_params=small(8),
        cost_estimate=pl.CostEstimate(flops=10**7, bytes_accessed=10**6, transcendentals=0),
    )(first, second, latter_filter_shift)

    pixels, to_inner, to_outer = pl.pallas_call(
        pick_kernel,
        out_shape=(
            jax.ShapeDtypeStruct((3, 2, ROWS, COLS), BF16),
            jax.ShapeDtypeStruct((ROWS, 128), BF16),
            jax.ShapeDtypeStruct((ROWS, 128), BF16),
        ),
        in_specs=[vmem()] * 2,
        out_specs=(vmem(),) * 3,
        compiler_params=small(8),
    )(picks, bands)

    inner = lax.ppermute(to_inner, "rng", [(i, i ^ 1) for i in range(rng_count)])
    partner = [i if i in (0, rng_count - 1) else ((i + 1) ^ 1) - 1 for i in range(rng_count)]
    outer = lax.ppermute(to_outer, "rng", list(enumerate(partner)))

    middle = pl.pallas_call(
        middle_kernel,
        out_shape=jax.ShapeDtypeStruct((2, 2, ROWS, COLS), F32),
        in_specs=[vmem()] * 5,
        out_specs=vmem(),
        scratch_shapes=[
            pltpu.VMEM((BLOCKS, 256, 2 * COLS), BF16),
            pltpu.VMEM((2, 80, 2 * COLS), F32),
        ],
        compiler_params=small(16),
        cost_estimate=pl.CostEstimate(flops=4 * 10**9, bytes_accessed=10**7, transcendentals=10**5),
    )(pixels, near, first_spread, second_spread, shift)

    return pl.pallas_call(
        edge_kernel,
        out_shape=jax.ShapeDtypeStruct((2, 2, ROWS, COLS), F32),
        in_specs=[vmem()] * 8,
        out_specs=vmem(),
        scratch_shapes=[
            pltpu.VMEM((3, 256, 512), BF16),
            pltpu.VMEM((2, 88, 512), F32),
        ],
        compiler_params=small(16),
    )(pixels, inner, outer, near, first_spread, second_spread, shift, middle)


def solution(mesh):
    placed = (P(None, None, "date", "rng"), P(None, "rng", None), P(), P(), P(), P(), P(), P())
    return jax.shard_map(
        local, mesh=mesh, in_specs=placed, out_specs=P("date", None, None, "rng"), check_vma=False
    )
```

```python
import jax
import jax.numpy as jnp
from jax import lax
from jax.experimental import pallas as pl
from jax.experimental.pallas import tpu as pltpu
from jax.sharding import PartitionSpec as P

BOX_AZ = 7
BOX_RG = 28
EPSILON = 1e-06
ROWS = 64
COLS = 256
BANDS = 16
EDGE = 16
STEP = 6
BLOCKS = 11
WINDOWS = 12
HIDDEN = 32
WIDE = STEP * HIDDEN
F32 = jnp.float32
BF16 = jnp.bfloat16


def iota(shape, dim):
    return lax.broadcasted_iota(jnp.int32, shape, dim)


def halves(value):
    high = value.astype(BF16)
    return high, (value - high.astype(F32)).astype(BF16)


def matmul(left, right):
    return jnp.dot(left, right, preferred_element_type=F32)


def send_kernel(chosen_ref, own_ref, sent_ref):
    chosen = chosen_ref[0]
    sent_ref[:, :2] = own_ref[...]
    master = own_ref[chosen // 2, chosen % 2]
    for band in range(BANDS):
        sent_ref[band, 2] = master


def spread_kernel(first_ref, second_ref, shift_ref, first_out, second_out, shift_out):
    row, col = iota((WIDE, 128), 0), iota((WIDE, 128), 1)
    tap = col % 8 - row // HIDDEN
    widen = (iota((WIDE, HIDDEN), 0) % HIDDEN == iota((WIDE, HIDDEN), 1)).astype(BF16)
    source, target = iota((48, 128), 0), iota((48, 128), 1)
    piece = target // 8
    shift = jnp.where(piece < 6, piece // 2, jnp.where(piece < 12, piece // 2 - 3, piece - 12))
    feature = jnp.where(piece < 6, piece % 2, jnp.where(piece < 12, 2 + piece % 2, 4))
    base = feature * 9 + shift
    offset = ((source == 45) & (target == 120)).astype(BF16)
    taken = [((source == base + 3 * a) & (piece < 15)).astype(BF16) for a in range(3)]
    for part, half in enumerate(halves(first_ref[...])):
        tall = matmul(widen, half).astype(BF16)
        spread = jnp.zeros((WIDE, 128), F32)
        for a in range(3):
            spread = jnp.where(tap == a, matmul(tall, taken[a]), spread)
        at = slice(WIDE * part, WIDE * part + WIDE)
        first_out[at, :128] = (spread + matmul(tall, offset)).astype(BF16)
        first_out[at, 128:] = (spread if part == 0 else jnp.zeros_like(spread)).astype(BF16)
    row, col = iota((48, WIDE), 0), iota((48, WIDE), 1)
    tap = col // HIDDEN + 2 - row % 8
    widen = (iota((HIDDEN, WIDE), 1) % HIDDEN == iota((HIDDEN, WIDE), 0)).astype(BF16)
    group, source = iota((48, 24), 0) // 8, iota((48, 24), 1)
    for part, half in enumerate(halves(second_ref[...])):
        wide = matmul(half, widen).astype(BF16)
        spread = jnp.zeros((48, WIDE), F32)
        for a in range(3):
            chosen = (source == group + 6 * a).astype(BF16)
            spread = jnp.where(tap == a, matmul(chosen, wide), spread)
        second_out[48 * part : 48 * part + 48, :] = spread.astype(BF16)
    for o in range(2):
        shift_out[o] = jnp.full((8, 128), shift_ref[o], F32)


def pick_kernel(chosen_ref, bands_ref, window_ref, inner_ref, outer_ref):
    odd = lax.axis_index("rng") % 2 == 1
    lane = iota((ROWS, 128), 1)
    first = jnp.zeros((ROWS, 128), F32)
    last = jnp.zeros((ROWS, 128), F32)
    for slot in range(3):
        for part in range(2):
            k = 2 * slot + part
            rows = bands_ref[:, slot, part].astype(F32).reshape(8 * BANDS, COLS).astype(BF16)
            picked = matmul(chosen_ref[slot], rows)
            window_ref[slot, part] = picked.astype(BF16)
            here = (lane >= EDGE * k) & (lane < EDGE * (k + 1))
            left = picked[:, :128]
            right = pltpu.roll(picked[:, 128:], EDGE * (k + 1), 1)
            if k:
                left = pltpu.roll(left, EDGE * k, 1)
            first = jnp.where(here, left, first)
            last = jnp.where(here, right, last)
    inner_ref[...] = jnp.where(odd, first, last).astype(BF16)
    outer_ref[...] = jnp.where(odd, last, first).astype(BF16)


def products(re, im):
    ref_re, ref_im = re[2], im[2]
    pow_ref = ref_re * ref_re + ref_im * ref_im
    planes = [pow_ref]
    for d in range(2):
        pow_sec = re[d] * re[d] + im[d] * im[d]
        planes += [
            pow_sec,
            ref_re * re[d] + ref_im * im[d],
            ref_im * re[d] - ref_re * im[d],
            jnp.sqrt(pow_ref * pow_sec),
        ]
    return planes


def sum_rows(summed, near_ref):
    return matmul(near_ref[...], jnp.concatenate(halves(summed), axis=0))


def mean_log(box_ref, inside):
    return jnp.where(inside, jnp.log(box_ref / (BOX_AZ * BOX_RG) + EPSILON), 0.0)


def features(box_ref, log_ref, boxed):
    inverse = 1.0 / (jnp.sqrt(box_ref * boxed[0]) + EPSILON)
    ratio = jnp.log(boxed[0] + EPSILON) - log_ref
    return boxed[1] * inverse, boxed[2] * inverse, boxed[3] * inverse, ratio


def window_rows(rows, base):
    row = iota(rows, 0)
    frame_row = row // 8 * STEP - 1 + row % 8 + base
    return (frame_row >= 0) & (frame_row < ROWS)


def sideways(value, b, span):
    if b == 1:
        return value
    width = value.shape[1]
    if span == width:
        return pltpu.roll(value, 1 if b == 0 else width - 1, 1)
    pieces = [sideways(value[:, at : at + span], b, span) for at in range(0, width, span)]
    return jnp.concatenate(pieces, axis=1)


def store_pieces(taps_ref, piece, upper, lower):
    for j in range(taps_ref.shape[0]):
        at = slice(8 * j, 8 * j + 8)
        high, low = halves(jnp.concatenate([upper[at], lower[at]], axis=0))
        taps_ref[j, 8 * piece : 8 * piece + 16, :] = high
        taps_ref[j, 128 + 8 * piece : 144 + 8 * piece, :] = low


def store_taps(taken, taps_ref, span):
    for pair in range(2):
        for b in range(3):
            upper, lower = [sideways(taken[2 * pair + k], b, span) for k in range(2)]
            store_pieces(taps_ref, 6 * pair + 2 * b, upper, lower)


def store_shared(shared, taps_refs, span):
    moved = [sideways(shared, b, span) for b in range(3)]
    one = jnp.where(iota(shared.shape, 0) % 8 == 0, 1.0, 0.0)
    for taps_ref in taps_refs:
        store_pieces(taps_ref, 12, moved[0], moved[1])
        store_pieces(taps_ref, 14, moved[2], one)


def first_part(taps, first_ref):
    doubled = matmul(first_ref[...], taps)
    return doubled[:WIDE] + doubled[WIDE:]


def second_part(sums, second_ref, keep):
    high, low = halves(keep(jnp.maximum(sums, 0.0)))
    doubled = matmul(second_ref[...], high)
    return doubled[:48] + doubled[48:] + matmul(second_ref[:48, :], low)


def class_window(parts, o, span):
    groups = [parts[16 * b + 8 * o : 16 * b + 8 * o + 8] for b in range(3)]
    return sum(sideways(groups[b], b, span) for b in range(3))


def carried(window, previous):
    if previous is None:
        return window
    row = iota(window.shape, 0)
    return window + jnp.where(row < 2, pltpu.roll(previous, 2, 0), 0.0)


def middle_kernel(window_ref, near_ref, first_ref, second_ref, shift_ref, out_ref, taps_ref, sum_ref):
    re = [window_ref[s, 0].astype(F32) for s in range(3)]
    im = [window_ref[s, 1].astype(F32) for s in range(3)]
    gap = iota((COLS, COLS), 0) - iota((COLS, COLS), 1) + BOX_RG // 2
    band = ((gap >= 0) & (gap < BOX_RG)).astype(BF16)
    planes = jnp.concatenate(products(re, im), axis=0)
    summed = matmul(jnp.concatenate(halves(planes), axis=1), jnp.concatenate([band, band], axis=0))
    live = 8 * BLOCKS
    boxed = [sum_rows(summed[ROWS * k : ROWS * k + ROWS], near_ref)[:live] for k in range(9)]
    log_ref = jnp.log(boxed[0] + EPSILON)
    shared = mean_log(boxed[0], window_rows((live, COLS), 0))
    sides = [taps_ref.at[:, :, COLS * d : COLS * d + COLS] for d in range(2)]
    store_shared(shared, sides, COLS)
    for d in range(2):
        store_taps(features(boxed[0], log_ref, boxed[1 + 4 * d : 5 + 4 * d]), sides[d], COLS)

    def keep(j):
        def masked(hidden):
            if j < BLOCKS - 1:
                return hidden
            row = iota(hidden.shape, 0)
            return jnp.where(row < (ROWS - STEP * j) * HIDDEN, hidden, 0.0)

        return masked

    previous = [None, None]
    ahead = first_part(taps_ref[0], first_ref)
    for j in range(BLOCKS):
        later = first_part(taps_ref[j + 1], first_ref) if j + 1 < BLOCKS else None
        parts = second_part(ahead, second_ref, keep(j))
        ahead = later
        for o in range(2):
            previous[o] = carried(class_window(parts, o, COLS), previous[o])
            sum_ref[o, STEP * j + 7 : STEP * j + 15, :] = previous[o]
    for d in range(2):
        for o in range(2):
            shift = jnp.concatenate([shift_ref[o], shift_ref[o]], axis=1)
            for k in range(8):
                done = sum_ref[o, 8 * k + 8 : 8 * k + 16, COLS * d : COLS * d + COLS]
                out_ref[d, o, 8 * k : 8 * k + 8, :] = done + shift


def edge_kernel(
    window_ref, inner_ref, outer_ref, near_ref, first_ref, second_ref, shift_ref, done_ref,
    out_ref, taps_ref, sum_ref,
):
    lane = iota((ROWS, 128), 1)
    place, places = lax.axis_index("rng"), lax.axis_size("rng")
    odd = place % 2 == 1
    inner, outer = inner_ref[...].astype(F32), outer_ref[...].astype(F32)
    before = jnp.where(place == 0, 0.0, jnp.where(odd, inner, outer))
    after = jnp.where(place == places - 1, 0.0, jnp.where(odd, outer, inner))

    def pixels(slot, part):
        k = 2 * slot + part
        value = window_ref[slot, part].astype(F32)
        own_first = pltpu.roll(value[:, :128], EDGE, 1)
        own_last = pltpu.roll(value[:, 128:], 96, 1)
        left = pltpu.roll(before, 128 - EDGE * k, 1) if k else before
        right = pltpu.roll(after, 96 - EDGE * k, 1)
        tile = jnp.where(lane < EDGE, left, own_first)
        tile = jnp.where(lane < 64, tile, own_last)
        tile = jnp.where(lane < 96, tile, right)
        return jnp.where(lane < 112, tile, 0.0)

    planes = products([pixels(s, 0) for s in range(3)], [pixels(s, 1) for s in range(3)])
    source, target = iota((128, 128), 0), iota((128, 128), 1)
    from_col = jnp.where(source < 64, source - 16, source + 160)
    side = target % 64 // 32
    to_col = target % 32 + jnp.where(side == 0, -4, 232)
    gap = from_col - to_col + BOX_RG // 2
    near = (gap >= 0) & (gap < BOX_RG) & (source // 64 == side)
    bands = [(near & (target // 64 == d)).astype(BF16) for d in range(2)]
    band = jnp.concatenate([bands[0], bands[0], bands[1], bands[1]], axis=0)
    dates = [jnp.concatenate([planes[0]] + planes[1 + 4 * d : 5 + 4 * d], axis=0) for d in range(2)]
    summed = matmul(jnp.concatenate(halves(dates[0]) + halves(dates[1]), axis=1), band)

    def spread(value):
        return jnp.concatenate([value[24 * q : 24 * q + 24] for q in range(4)], axis=1)

    boxed = [spread(sum_rows(summed[ROWS * k : ROWS * k + ROWS], near_ref)) for k in range(5)]

    def in_frame(rows):
        spot = iota((rows, 512), 1)
        column = spot % 32 + jnp.where(spot % 64 < 32, -4, 232)
        low = jnp.where(place == 0, 0, -128)
        high = jnp.where(place == places - 1, COLS, 2 * COLS)
        return (column >= low) & (column < high)

    valid = in_frame(24)
    base = iota((24, 512), 1) // 128 * (3 * STEP)
    shared = mean_log(boxed[0], window_rows((24, 512), base) & valid)
    store_shared(shared, [taps_ref], 128)
    taken = features(boxed[0], jnp.log(boxed[0] + EPSILON), boxed[1:])
    store_taps([jnp.where(valid, f, 0.0) for f in taken], taps_ref, 128)
    kept = in_frame(WIDE)
    row, spot = iota((WIDE, 512), 0), iota((WIDE, 512), 1)
    ended = kept & ((spot < 384) | (row < 4 * HIDDEN))
    sum_ref[...] = jnp.zeros_like(sum_ref)
    previous = [None, None]
    ahead = first_part(taps_ref[0], first_ref)
    for j in range(3):
        later = first_part(taps_ref[j + 1], first_ref) if j < 2 else None
        mask = ended if j == 1 else kept
        parts = second_part(ahead, second_ref, lambda hidden: jnp.where(mask, hidden, 0.0))
        ahead = later
        for o in range(2):
            previous[o] = carried(class_window(parts, o, 128), previous[o])
            for q in range(4):
                at, lanes = STEP * (j + 3 * q) + 7, slice(128 * q, 128 * q + 128)
                sum_ref[o, at : at + 8, lanes] = previous[o][:, lanes]
    spot = iota((8, 128), 1)
    for k in range(8):
        at, to = slice(8 * k + 8, 8 * k + 16), slice(8 * k, 8 * k + 8)
        for o in range(2):
            value = sum(sum_ref[o, at, 128 * q : 128 * q + 128] for q in range(4)) + shift_ref[o]
            for d in range(2):
                left = pltpu.roll(value, 128 - 64 * d - 4, 1)
                right = pltpu.roll(value, (112 - 64 * d - 40) % 128, 1)
                out_ref[d, o, to, :128] = jnp.where(spot < EDGE, left, done_ref[d, o, to, :128])
                out_ref[d, o, to, 128:] = jnp.where(spot >= 112, right, done_ref[d, o, to, 128:])


def vmem():
    return pl.BlockSpec(memory_space=pltpu.VMEM)


def smem():
    return pl.BlockSpec(memory_space=pltpu.SMEM)


def small(mib):
    return pltpu.CompilerParams(vmem_limit_bytes=mib << 20)


def local(
    slave_complex_pixels,
    along_track_line_groups,
    master_epoch_position,
    sweep_identifier,
    initial_filter_kernel,
    initial_filter_shift,
    latter_filter_kernel,
    latter_filter_shift,
):
    date_index = lax.axis_index("date")
    rng_count = lax.axis_size("rng")
    chosen = master_epoch_position[0]
    sent = pl.pallas_call(
        send_kernel,
        out_shape=jax.ShapeDtypeStruct((BANDS, 3, 2, 8, COLS), BF16),
        in_specs=[smem(), vmem()],
        out_specs=vmem(),
        compiler_params=small(4),
    )(master_epoch_position, slave_complex_pixels.reshape(BANDS, 2, 2, 8, COLS))
    bands = lax.all_to_all(sent, "date", split_axis=0, concat_axis=0, tiled=True)

    lists = along_track_line_groups[:, 0, :]
    mine = lax.dynamic_slice_in_dim(lists, date_index * 2, 2, 0)
    lists = jnp.concatenate([mine, lax.dynamic_slice_in_dim(lists, chosen, 1, 0)], axis=0)
    row_of = lax.broadcasted_iota(jnp.int32, (3, ROWS, 8 * BANDS), 2)
    picks = (lists[:, :, None] == row_of).astype(BF16)

    window = jnp.arange(8 * WINDOWS)
    frame_row = window // 8 * STEP - 1 + window % 8
    row_id = jnp.arange(ROWS)
    burst = sweep_identifier.astype(jnp.int32)
    target_burst = jnp.sum(jnp.where(frame_row[:, None] == row_id[None, :], burst[None, :], 0), axis=1)
    near = (
        (jnp.abs(row_id[None, :] - frame_row[:, None]) <= BOX_AZ // 2)
        & (burst[None, :] == target_burst[:, None])
        & (frame_row >= 0)[:, None]
        & (frame_row < ROWS)[:, None]
    ).astype(BF16)
    near = jnp.concatenate([near, near], axis=1)

    first = jnp.concatenate(
        [
            initial_filter_kernel.reshape(HIDDEN, 45),
            initial_filter_shift[:, None],
            jnp.zeros((HIDDEN, 2), F32),
        ],
        axis=1,
    )
    second = jnp.pad(
        jnp.transpose(latter_filter_kernel, (2, 3, 0, 1)).reshape(18, HIDDEN), ((0, 6), (0, 0))
    )
    first_spread, second_spread, shift = pl.pallas_call(
        spread_kernel,
        out_shape=(
            jax.ShapeDtypeStruct((2 * WIDE, COLS), BF16),
            jax.ShapeDtypeStruct((96, WIDE), BF16),
            jax.ShapeDtypeStruct((2, 8, 128), F32),
        ),
        in_specs=[vmem()] * 2 + [smem()],
        out_specs=(vmem(),) * 3,
        compiler_params=small(8),
        cost_estimate=pl.CostEstimate(flops=10**7, bytes_accessed=10**6, transcendentals=0),
    )(first, second, latter_filter_shift)

    pixels, to_inner, to_outer = pl.pallas_call(
        pick_kernel,
        out_shape=(
            jax.ShapeDtypeStruct((3, 2, ROWS, COLS), BF16),
            jax.ShapeDtypeStruct((ROWS, 128), BF16),
            jax.ShapeDtypeStruct((ROWS, 128), BF16),
        ),
        in_specs=[vmem()] * 2,
        out_specs=(vmem(),) * 3,
        compiler_params=small(8),
    )(picks, bands)

    inner = lax.ppermute(to_inner, "rng", [(i, i ^ 1) for i in range(rng_count)])
    swaps = []
    for d in range(lax.axis_size("date")):
        for i in range(rng_count):
            across = (d ^ 1, i) if i in (0, rng_count - 1) else (d, ((i + 1) ^ 1) - 1)
            swaps.append((d * rng_count + i, across[0] * rng_count + across[1]))
    outer = lax.ppermute(to_outer, ("date", "rng"), swaps)

    middle = pl.pallas_call(
        middle_kernel,
        out_shape=jax.ShapeDtypeStruct((2, 2, ROWS, COLS), F32),
        in_specs=[vmem()] * 5,
        out_specs=vmem(),
        scratch_shapes=[
            pltpu.VMEM((BLOCKS, 256, 2 * COLS), BF16),
            pltpu.VMEM((2, 80, 2 * COLS), F32),
        ],
        compiler_params=small(16),
        cost_estimate=pl.CostEstimate(flops=4 * 10**9, bytes_accessed=10**7, transcendentals=10**5),
    )(pixels, near, first_spread, second_spread, shift)

    return pl.pallas_call(
        edge_kernel,
        out_shape=jax.ShapeDtypeStruct((2, 2, ROWS, COLS), F32),
        in_specs=[vmem()] * 8,
        out_specs=vmem(),
        scratch_shapes=[
            pltpu.VMEM((3, 256, 512), BF16),
            pltpu.VMEM((2, 88, 512), F32),
        ],
        compiler_params=small(16),
    )(pixels, inner, outer, near, first_spread, second_spread, shift, middle)


def solution(mesh):
    placed = (P(None, None, "date", "rng"), P(None, "rng", None), P(), P(), P(), P(), P(), P())
    return jax.shard_map(
        local, mesh=mesh, in_specs=placed, out_specs=P("date", None, None, "rng"), check_vma=False
    )
```

```python
import jax
import jax.numpy as jnp
from jax import lax
from jax.experimental import pallas as pl
from jax.experimental.pallas import tpu as pltpu
from jax.sharding import PartitionSpec as P

BOX_AZ = 7
BOX_RG = 28
EPSILON = 1e-06
ROWS = 64
COLS = 256
BANDS = 16
EDGE = 16
STEP = 6
BLOCKS = 11
WINDOWS = 12
HIDDEN = 32
WIDE = STEP * HIDDEN
F32 = jnp.float32
BF16 = jnp.bfloat16


def iota(shape, dim):
    return lax.broadcasted_iota(jnp.int32, shape, dim)


def halves(value):
    high = value.astype(BF16)
    return high, (value - high.astype(F32)).astype(BF16)


def matmul(left, right):
    return jnp.dot(left, right, preferred_element_type=F32)


def send_kernel(chosen_ref, own_ref, sent_ref):
    chosen = chosen_ref[0]
    sent_ref[:, :2] = own_ref[...]
    master = own_ref[chosen // 2, chosen % 2]
    for band in range(BANDS):
        sent_ref[band, 2] = master


def spread_kernel(first_ref, second_ref, shift_ref, first_out, second_out, shift_out, band_out, edge_out):
    gap = iota((COLS, COLS), 0) - iota((COLS, COLS), 1) + BOX_RG // 2
    band_out[...] = ((gap >= 0) & (gap < BOX_RG)).astype(BF16)
    source, target = iota((128, 128), 0), iota((128, 128), 1)
    from_col = jnp.where(source < 64, source - 16, source + 160)
    side = target % 64 // 32
    to_col = target % 32 + jnp.where(side == 0, -4, 232)
    gap = from_col - to_col + BOX_RG // 2
    near = (gap >= 0) & (gap < BOX_RG) & (source // 64 == side)
    for d in range(2):
        edge_out[d] = (near & (target // 64 == d)).astype(BF16)
    row, col = iota((WIDE, 128), 0), iota((WIDE, 128), 1)
    tap = col % 8 - row // HIDDEN
    widen = (iota((WIDE, HIDDEN), 0) % HIDDEN == iota((WIDE, HIDDEN), 1)).astype(BF16)
    source, target = iota((48, 128), 0), iota((48, 128), 1)
    piece = target // 8
    shift = jnp.where(piece < 6, piece // 2, jnp.where(piece < 12, piece // 2 - 3, piece - 12))
    feature = jnp.where(piece < 6, piece % 2, jnp.where(piece < 12, 2 + piece % 2, 4))
    base = feature * 9 + shift
    offset = ((source == 45) & (target == 120)).astype(BF16)
    taken = [((source == base + 3 * a) & (piece < 15)).astype(BF16) for a in range(3)]
    for part, half in enumerate(halves(first_ref[...])):
        tall = matmul(widen, half).astype(BF16)
        spread = jnp.zeros((WIDE, 128), F32)
        for a in range(3):
            spread = jnp.where(tap == a, matmul(tall, taken[a]), spread)
        at = slice(WIDE * part, WIDE * part + WIDE)
        first_out[at, :128] = (spread + matmul(tall, offset)).astype(BF16)
        first_out[at, 128:] = (spread if part == 0 else jnp.zeros_like(spread)).astype(BF16)
    row, col = iota((48, WIDE), 0), iota((48, WIDE), 1)
    tap = col // HIDDEN + 2 - row % 8
    widen = (iota((HIDDEN, WIDE), 1) % HIDDEN == iota((HIDDEN, WIDE), 0)).astype(BF16)
    group, source = iota((48, 24), 0) // 8, iota((48, 24), 1)
    for part, half in enumerate(halves(second_ref[...])):
        wide = matmul(half, widen).astype(BF16)
        spread = jnp.zeros((48, WIDE), F32)
        for a in range(3):
            chosen = (source == group + 6 * a).astype(BF16)
            spread = jnp.where(tap == a, matmul(chosen, wide), spread)
        second_out[48 * part : 48 * part + 48, :] = spread.astype(BF16)
    for o in range(2):
        shift_out[o] = jnp.full((8, 128), shift_ref[o], F32)


def pick_kernel(chosen_ref, bands_ref, window_ref, inner_ref, outer_ref):
    odd = lax.axis_index("rng") % 2 == 1
    lane = iota((ROWS, 128), 1)
    first = jnp.zeros((ROWS, 128), F32)
    last = jnp.zeros((ROWS, 128), F32)
    for slot in range(3):
        for part in range(2):
            k = 2 * slot + part
            rows = bands_ref[:, slot, part].astype(F32).reshape(8 * BANDS, COLS).astype(BF16)
            picked = matmul(chosen_ref[slot], rows)
            window_ref[slot, part] = picked.astype(BF16)
            here = (lane >= EDGE * k) & (lane < EDGE * (k + 1))
            left = picked[:, :128]
            right = pltpu.roll(picked[:, 128:], EDGE * (k + 1), 1)
            if k:
                left = pltpu.roll(left, EDGE * k, 1)
            first = jnp.where(here, left, first)
            last = jnp.where(here, right, last)
    inner_ref[...] = jnp.where(odd, first, last).astype(BF16)
    outer_ref[...] = jnp.where(odd, last, first).astype(BF16)


def products(re, im):
    ref_re, ref_im = re[2], im[2]
    pow_ref = ref_re * ref_re + ref_im * ref_im
    planes = [pow_ref]
    for d in range(2):
        pow_sec = re[d] * re[d] + im[d] * im[d]
        planes += [
            pow_sec,
            ref_re * re[d] + ref_im * im[d],
            ref_im * re[d] - ref_re * im[d],
            jnp.sqrt(pow_ref * pow_sec),
        ]
    return planes


def sum_rows(summed, near_ref):
    return matmul(near_ref[...], jnp.concatenate(halves(summed), axis=0))


def mean_log(box_ref, inside):
    return jnp.where(inside, jnp.log(box_ref / (BOX_AZ * BOX_RG) + EPSILON), 0.0)


def features(box_ref, log_ref, boxed):
    inverse = 1.0 / (jnp.sqrt(box_ref * boxed[0]) + EPSILON)
    ratio = jnp.log(boxed[0] + EPSILON) - log_ref
    return boxed[1] * inverse, boxed[2] * inverse, boxed[3] * inverse, ratio


def window_rows(rows, base):
    row = iota(rows, 0)
    frame_row = row // 8 * STEP - 1 + row % 8 + base
    return (frame_row >= 0) & (frame_row < ROWS)


def sideways(value, b, span):
    if b == 1:
        return value
    width = value.shape[1]
    if span == width:
        return pltpu.roll(value, 1 if b == 0 else width - 1, 1)
    pieces = [sideways(value[:, at : at + span], b, span) for at in range(0, width, span)]
    return jnp.concatenate(pieces, axis=1)


def store_pieces(taps_ref, piece, upper, lower):
    for j in range(taps_ref.shape[0]):
        at = slice(8 * j, 8 * j + 8)
        high, low = halves(jnp.concatenate([upper[at], lower[at]], axis=0))
        taps_ref[j, 8 * piece : 8 * piece + 16, :] = high
        taps_ref[j, 128 + 8 * piece : 144 + 8 * piece, :] = low


def store_taps(taken, taps_ref, span):
    for pair in range(2):
        for b in range(3):
            upper, lower = [sideways(taken[2 * pair + k], b, span) for k in range(2)]
            store_pieces(taps_ref, 6 * pair + 2 * b, upper, lower)


def store_shared(shared, taps_refs, span):
    moved = [sideways(shared, b, span) for b in range(3)]
    one = jnp.where(iota(shared.shape, 0) % 8 == 0, 1.0, 0.0)
    for taps_ref in taps_refs:
        store_pieces(taps_ref, 12, moved[0], moved[1])
        store_pieces(taps_ref, 14, moved[2], one)


def first_part(taps, first_ref):
    doubled = matmul(first_ref[...], taps)
    return doubled[:WIDE] + doubled[WIDE:]


def second_part(sums, second_ref, keep):
    high, low = halves(keep(jnp.maximum(sums, 0.0)))
    doubled = matmul(second_ref[...], high)
    return doubled[:48] + doubled[48:] + matmul(second_ref[:48, :], low)


def class_window(parts, o, span):
    groups = [parts[16 * b + 8 * o : 16 * b + 8 * o + 8] for b in range(3)]
    return sum(sideways(groups[b], b, span) for b in range(3))


def carried(window, previous):
    if previous is None:
        return window
    row = iota(window.shape, 0)
    return window + jnp.where(row < 2, pltpu.roll(previous, 2, 0), 0.0)


def middle_kernel(window_ref, near_ref, first_ref, second_ref, shift_ref, band_ref, out_ref, taps_ref, sum_ref):
    re = [window_ref[s, 0].astype(F32) for s in range(3)]
    im = [window_ref[s, 1].astype(F32) for s in range(3)]
    band = band_ref[...]
    planes = jnp.concatenate(products(re, im), axis=0)
    summed = matmul(jnp.concatenate(halves(planes), axis=1), jnp.concatenate([band, band], axis=0))
    live = 8 * BLOCKS
    boxed = [sum_rows(summed[ROWS * k : ROWS * k + ROWS], near_ref)[:live] for k in range(9)]
    log_ref = jnp.log(boxed[0] + EPSILON)
    shared = mean_log(boxed[0], window_rows((live, COLS), 0))
    sides = [taps_ref.at[:, :, COLS * d : COLS * d + COLS] for d in range(2)]
    store_shared(shared, sides, COLS)
    for d in range(2):
        store_taps(features(boxed[0], log_ref, boxed[1 + 4 * d : 5 + 4 * d]), sides[d], COLS)

    def keep(j):
        def masked(hidden):
            if j < BLOCKS - 1:
                return hidden
            row = iota(hidden.shape, 0)
            return jnp.where(row < (ROWS - STEP * j) * HIDDEN, hidden, 0.0)

        return masked

    previous = [None, None]
    ahead = first_part(taps_ref[0], first_ref)
    for j in range(BLOCKS):
        later = first_part(taps_ref[j + 1], first_ref) if j + 1 < BLOCKS else None
        parts = second_part(ahead, second_ref, keep(j))
        ahead = later
        for o in range(2):
            previous[o] = carried(class_window(parts, o, COLS), previous[o])
            sum_ref[o, STEP * j + 7 : STEP * j + 15, :] = previous[o]
    for d in range(2):
        for o in range(2):
            shift = jnp.concatenate([shift_ref[o], shift_ref[o]], axis=1)
            for k in range(8):
                done = sum_ref[o, 8 * k + 8 : 8 * k + 16, COLS * d : COLS * d + COLS]
                out_ref[d, o, 8 * k : 8 * k + 8, :] = done + shift


def edge_kernel(
    window_ref, inner_ref, outer_ref, near_ref, first_ref, second_ref, shift_ref, band_ref, done_ref,
    out_ref, taps_ref, sum_ref,
):
    lane = iota((ROWS, 128), 1)
    place, places = lax.axis_index("rng"), lax.axis_size("rng")
    odd = place % 2 == 1
    inner, outer = inner_ref[...].astype(F32), outer_ref[...].astype(F32)
    before = jnp.where(place == 0, 0.0, jnp.where(odd, inner, outer))
    after = jnp.where(place == places - 1, 0.0, jnp.where(odd, outer, inner))

    def pixels(slot, part):
        k = 2 * slot + part
        value = window_ref[slot, part].astype(F32)
        own_first = pltpu.roll(value[:, :128], EDGE, 1)
        own_last = pltpu.roll(value[:, 128:], 96, 1)
        left = pltpu.roll(before, 128 - EDGE * k, 1) if k else before
        right = pltpu.roll(after, 96 - EDGE * k, 1)
        tile = jnp.where(lane < EDGE, left, own_first)
        tile = jnp.where(lane < 64, tile, own_last)
        tile = jnp.where(lane < 96, tile, right)
        return jnp.where(lane < 112, tile, 0.0)

    planes = products([pixels(s, 0) for s in range(3)], [pixels(s, 1) for s in range(3)])
    bands = [band_ref[d] for d in range(2)]
    band = jnp.concatenate([bands[0], bands[0], bands[1], bands[1]], axis=0)
    dates = [jnp.concatenate([planes[0]] + planes[1 + 4 * d : 5 + 4 * d], axis=0) for d in range(2)]
    summed = matmul(jnp.concatenate(halves(dates[0]) + halves(dates[1]), axis=1), band)

    def spread(value):
        return jnp.concatenate([value[24 * q : 24 * q + 24] for q in range(4)], axis=1)

    boxed = [spread(sum_rows(summed[ROWS * k : ROWS * k + ROWS], near_ref)) for k in range(5)]

    def in_frame(rows):
        spot = iota((rows, 512), 1)
        column = spot % 32 + jnp.where(spot % 64 < 32, -4, 232)
        low = jnp.where(place == 0, 0, -128)
        high = jnp.where(place == places - 1, COLS, 2 * COLS)
        return (column >= low) & (column < high)

    valid = in_frame(24)
    base = iota((24, 512), 1) // 128 * (3 * STEP)
    shared = mean_log(boxed[0], window_rows((24, 512), base) & valid)
    store_shared(shared, [taps_ref], 128)
    taken = features(boxed[0], jnp.log(boxed[0] + EPSILON), boxed[1:])
    store_taps([jnp.where(valid, f, 0.0) for f in taken], taps_ref, 128)
    kept = in_frame(WIDE)
    row, spot = iota((WIDE, 512), 0), iota((WIDE, 512), 1)
    ended = kept & ((spot < 384) | (row < 4 * HIDDEN))
    sum_ref[...] = jnp.zeros_like(sum_ref)
    previous = [None, None]
    ahead = first_part(taps_ref[0], first_ref)
    for j in range(3):
        later = first_part(taps_ref[j + 1], first_ref) if j < 2 else None
        mask = ended if j == 1 else kept
        parts = second_part(ahead, second_ref, lambda hidden: jnp.where(mask, hidden, 0.0))
        ahead = later
        for o in range(2):
            previous[o] = carried(class_window(parts, o, 128), previous[o])
            for q in range(4):
                at, lanes = STEP * (j + 3 * q) + 7, slice(128 * q, 128 * q + 128)
                sum_ref[o, at : at + 8, lanes] = previous[o][:, lanes]
    spot = iota((8, 128), 1)
    for k in range(8):
        at, to = slice(8 * k + 8, 8 * k + 16), slice(8 * k, 8 * k + 8)
        for o in range(2):
            value = sum(sum_ref[o, at, 128 * q : 128 * q + 128] for q in range(4)) + shift_ref[o]
            for d in range(2):
                left = pltpu.roll(value, 128 - 64 * d - 4, 1)
                right = pltpu.roll(value, (112 - 64 * d - 40) % 128, 1)
                out_ref[d, o, to, :128] = jnp.where(spot < EDGE, left, done_ref[d, o, to, :128])
                out_ref[d, o, to, 128:] = jnp.where(spot >= 112, right, done_ref[d, o, to, 128:])


def vmem():
    return pl.BlockSpec(memory_space=pltpu.VMEM)


def smem():
    return pl.BlockSpec(memory_space=pltpu.SMEM)


def small(mib):
    return pltpu.CompilerParams(vmem_limit_bytes=mib << 20)


def local(
    slave_complex_pixels,
    along_track_line_groups,
    master_epoch_position,
    sweep_identifier,
    initial_filter_kernel,
    initial_filter_shift,
    latter_filter_kernel,
    latter_filter_shift,
):
    date_index = lax.axis_index("date")
    rng_count = lax.axis_size("rng")
    chosen = master_epoch_position[0]
    sent = pl.pallas_call(
        send_kernel,
        out_shape=jax.ShapeDtypeStruct((BANDS, 3, 2, 8, COLS), BF16),
        in_specs=[smem(), vmem()],
        out_specs=vmem(),
        compiler_params=small(4),
    )(master_epoch_position, slave_complex_pixels.reshape(BANDS, 2, 2, 8, COLS))
    bands = lax.all_to_all(sent, "date", split_axis=0, concat_axis=0, tiled=True)

    lists = along_track_line_groups[:, 0, :]
    mine = lax.dynamic_slice_in_dim(lists, date_index * 2, 2, 0)
    lists = jnp.concatenate([mine, lax.dynamic_slice_in_dim(lists, chosen, 1, 0)], axis=0)
    row_of = lax.broadcasted_iota(jnp.int32, (3, ROWS, 8 * BANDS), 2)
    picks = (lists[:, :, None] == row_of).astype(BF16)

    window = jnp.arange(8 * WINDOWS)
    frame_row = window // 8 * STEP - 1 + window % 8
    row_id = jnp.arange(ROWS)
    burst = sweep_identifier.astype(jnp.int32)
    target_burst = jnp.sum(jnp.where(frame_row[:, None] == row_id[None, :], burst[None, :], 0), axis=1)
    near = (
        (jnp.abs(row_id[None, :] - frame_row[:, None]) <= BOX_AZ // 2)
        & (burst[None, :] == target_burst[:, None])
        & (frame_row >= 0)[:, None]
        & (frame_row < ROWS)[:, None]
    ).astype(BF16)
    near = jnp.concatenate([near, near], axis=1)

    first = jnp.concatenate(
        [
            initial_filter_kernel.reshape(HIDDEN, 45),
            initial_filter_shift[:, None],
            jnp.zeros((HIDDEN, 2), F32),
        ],
        axis=1,
    )
    second = jnp.pad(
        jnp.transpose(latter_filter_kernel, (2, 3, 0, 1)).reshape(18, HIDDEN), ((0, 6), (0, 0))
    )
    first_spread, second_spread, shift, band, edge_band = pl.pallas_call(
        spread_kernel,
        out_shape=(
            jax.ShapeDtypeStruct((2 * WIDE, COLS), BF16),
            jax.ShapeDtypeStruct((96, WIDE), BF16),
            jax.ShapeDtypeStruct((2, 8, 128), F32),
            jax.ShapeDtypeStruct((COLS, COLS), BF16),
            jax.ShapeDtypeStruct((2, 128, 128), BF16),
        ),
        in_specs=[vmem()] * 2 + [smem()],
        out_specs=(vmem(),) * 5,
        compiler_params=small(8),
        cost_estimate=pl.CostEstimate(flops=10**7, bytes_accessed=10**6, transcendentals=0),
    )(first, second, latter_filter_shift)

    pixels, to_inner, to_outer = pl.pallas_call(
        pick_kernel,
        out_shape=(
            jax.ShapeDtypeStruct((3, 2, ROWS, COLS), BF16),
            jax.ShapeDtypeStruct((ROWS, 128), BF16),
            jax.ShapeDtypeStruct((ROWS, 128), BF16),
        ),
        in_specs=[vmem()] * 2,
        out_specs=(vmem(),) * 3,
        compiler_params=small(8),
    )(picks, bands)

    inner = lax.ppermute(to_inner, "rng", [(i, i ^ 1) for i in range(rng_count)])
    swaps = []
    for d in range(lax.axis_size("date")):
        for i in range(rng_count):
            across = (d ^ 1, i) if i in (0, rng_count - 1) else (d, ((i + 1) ^ 1) - 1)
            swaps.append((d * rng_count + i, across[0] * rng_count + across[1]))
    outer = lax.ppermute(to_outer, ("date", "rng"), swaps)

    middle = pl.pallas_call(
        middle_kernel,
        out_shape=jax.ShapeDtypeStruct((2, 2, ROWS, COLS), F32),
        in_specs=[vmem()] * 6,
        out_specs=vmem(),
        scratch_shapes=[
            pltpu.VMEM((BLOCKS, 256, 2 * COLS), BF16),
            pltpu.VMEM((2, 80, 2 * COLS), F32),
        ],
        compiler_params=small(16),
        cost_estimate=pl.CostEstimate(flops=4 * 10**9, bytes_accessed=10**7, transcendentals=10**5),
    )(pixels, near, first_spread, second_spread, shift, band)

    return pl.pallas_call(
        edge_kernel,
        out_shape=jax.ShapeDtypeStruct((2, 2, ROWS, COLS), F32),
        in_specs=[vmem()] * 9,
        out_specs=vmem(),
        scratch_shapes=[
            pltpu.VMEM((3, 256, 512), BF16),
            pltpu.VMEM((2, 88, 512), F32),
        ],
        compiler_params=small(16),
    )(pixels, inner, outer, near, first_spread, second_spread, shift, edge_band, middle)


def solution(mesh):
    placed = (P(None, None, "date", "rng"), P(None, "rng", None), P(), P(), P(), P(), P(), P())
    return jax.shard_map(
        local, mesh=mesh, in_specs=placed, out_specs=P("date", None, None, "rng"), check_vma=False
    )
```
